32 devices in a mesh: groups: 1, row: 16 (over z, y, core), col: 2 (over x).
Axes of the slice: x: 2, y: 2, z: 4, core: 2. Of those that a mesh axis runs over, the one named last changes fastest.
Arguments:
- pair_grid: bfloat16 [256, 256, 128], P(('groups', 'row'), 'col'), may hold values from -6 to 6
- alignment_pool: bfloat16 [256, 256, 64], P('groups', 'row'), may hold values from -6 to 6
- sample_index: int32 [64], P('groups'), may hold values from 0 to 255
- token_mask: int32 [256], P('groups'), may hold values 0 or 1
- outer_proj: bfloat16 [64, 64], replicated, may hold values from -0.75 to 0.75
- outer_mix: bfloat16 [1024, 128], replicated, may hold values from -0.375 to 0.375
- pair_logit: bfloat16 [128, 8], replicated, may hold values from -1 to 1
- average_proj: bfloat16 [64, 512], replicated, may hold values from -0.75 to 0.75
- average_mix: bfloat16 [256, 64], replicated, may hold values from -0.75 to 0.75
- triangle_proj: bfloat16 [128, 640], replicated, may hold values from -0.5 to 0.5
- triangle_mix: bfloat16 [128, 128], replicated, may hold values from -0.5 to 0.5
- transition_up: bfloat16 [128, 1024], replicated, may hold values from -0.5 to 0.5
- transition_down: bfloat16 [512, 128], replicated, may hold values from -0.25 to 0.25
Outputs:
- pair_next: bfloat16 [256, 256, 128], P(('groups', 'row'), 'col')
- alignment_next: bfloat16 [64, 256, 64], P('groups', 'row')
The draws below stay inside these ranges and needn't reach their ends.
Inputs may be any that keep to these rules, and one draw needn't show every extreme that they name: `sample_index`: indices into the first dimension of alignment_pool; they may repeat. `token_mask`: 1 marks a real residue, 0 a padded one.
All inputs are finite; a program needn't handle non-finite values.
Results may differ from the reference program's by a relative error of at most 0.008.
Values may be sent and summed in bfloat16 or wider, within the bound.
A program may use at most 64 MiB of HBM per device.

```python
import math
import jax
import jax.numpy as jnp
from jax import lax

C = 128
CM = 64
OPC = 32
H = 8
HC = 32
TR = 512
S = 64
POOL = 256
N = 256


def with_ends(drawn, stream_key, least, top_value):
    spot = [jax.random.randint(jax.random.fold_in(stream_key, axis), (), 0, length) for axis, length in enumerate(drawn.shape)]
    main_axis = drawn.shape.index(max(drawn.shape))
    beside = spot[:main_axis] + [(spot[main_axis] + 1) % drawn.shape[main_axis]] + spot[main_axis + 1:]
    return drawn.at[tuple(spot)].set(least).at[tuple(beside)].set(top_value)


def steps_of(rng, dims, pieces, low, largest):
    level, own = 1.0, jax.random.fold_in(rng, 6)
    for axis_at, shards_of in pieces:
        heights = jnp.exp(jax.random.uniform(jax.random.fold_in(own, axis_at), (shards_of,), jnp.float32, low / len(pieces), largest / len(pieces)))
        level = level * jnp.repeat(heights, dims[axis_at] // shards_of).reshape([-1 if axis == axis_at else 1 for axis in range(len(dims))])
    return level


def normal_values(stream_key, extent, scale, bound, shards=(), kind=jnp.bfloat16):
    gain = steps_of(stream_key, extent, shards, -0.22, 0.18) if shards else 1.0
    array = jax.random.normal(stream_key, extent, jnp.float32) * scale * gain
    return jnp.minimum(jnp.maximum(array, -bound), bound).astype(kind)


def setup_inputs(seed: int = 0, part: int = 0) -> dict:
    splits = jax.random.split(jax.random.key(seed), 14)
    part_keys = jax.random.split(jax.random.fold_in(splits[13], part), 14)
    pair_grid = normal_values(part_keys[0], (N, N, C), 1.0, 6.0, ((0, 16), (1, 2)))
    alignment_pool = normal_values(part_keys[1], (POOL, N, CM), 1.0, 6.0, ((1, 16),))
    sample_index = with_ends(jax.random.randint(part_keys[2], (S,), 0, POOL), jax.random.fold_in(part_keys[2], 1), 0, POOL - 1).astype(jnp.int32)
    token_mask = with_ends((jax.random.randint(part_keys[3], (N,), 0, 8) < 7).astype(jnp.int32), jax.random.fold_in(part_keys[3], 1), 0, 1)
    outer_proj = normal_values(splits[4], (CM, 2 * OPC), CM ** -0.5, 0.75)
    outer_mix = normal_values(splits[5], (OPC * OPC, C), (OPC * OPC // 4) ** -0.5, 0.375)
    pair_logit = normal_values(splits[6], (C, H), (C // 4) ** -0.5, 1.0)
    average_proj = normal_values(splits[7], (CM, 2 * H * HC), CM ** -0.5, 0.75)
    average_mix = normal_values(splits[8], (H * HC, CM), (H * HC // 4) ** -0.5, 0.75)
    triangle_proj = normal_values(splits[9], (C, 5 * C), C ** -0.5, 0.5)
    triangle_mix = normal_values(splits[10], (C, C), C ** -0.5, 0.5)
    transition_up = normal_values(splits[11], (C, 2 * TR), C ** -0.5, 0.5)
    transition_down = normal_values(splits[12], (TR, C), TR ** -0.5, 0.25)
    return dict(pair_grid=pair_grid, alignment_pool=alignment_pool, sample_index=sample_index, token_mask=token_mask, outer_proj=outer_proj, outer_mix=outer_mix, pair_logit=pair_logit, average_proj=average_proj, average_mix=average_mix, triangle_proj=triangle_proj, triangle_mix=triangle_mix, transition_up=transition_up, transition_down=transition_down)


epsilon = 1e-05

def normalize(values, channel_dim):
    values = values.astype(jnp.float32)
    centred = values - lax.optimization_barrier(jnp.mean(values, axis=channel_dim, keepdims=True))
    spread = lax.optimization_barrier(jnp.mean(centred * centred, axis=channel_dim, keepdims=True))
    return centred / jnp.sqrt(spread + epsilon)

def settle_wide(values):
    return lax.optimization_barrier(values).astype(jnp.float32)

def reference(pair_grid, alignment_pool, sample_index, token_mask, outer_proj, outer_mix, pair_logit, average_proj, average_mix, triangle_proj, triangle_mix, transition_up, transition_down):
    alignments = jnp.take(alignment_pool, sample_index, axis=0)
    align_norm = normalize(alignments, 2).astype(jnp.bfloat16)
    align_flat = align_norm.reshape(S * N, CM)
    row_factor = jnp.dot(align_flat, outer_proj[:, :OPC], preferred_element_type=jnp.float32).astype(jnp.bfloat16).reshape(S, N, OPC)
    column_factor = jnp.dot(align_flat, outer_proj[:, OPC:], preferred_element_type=jnp.float32).astype(jnp.bfloat16).reshape(S, N, OPC)
    column_wide = settle_wide(column_factor)
    block_rows = math.gcd(N, 32)
    start_rows = (jnp.arange(N // block_rows) * block_rows).astype(jnp.int32)

    def outer_step(first_row):
        left_block = settle_wide(lax.dynamic_slice_in_dim(row_factor, first_row, block_rows, 1))
        outer_sum = jnp.einsum('sic,sjd->ijcd', left_block, column_wide)
        outer_mean = (outer_sum * (1.0 / S)).astype(jnp.bfloat16).reshape(block_rows * N, OPC * OPC)
        pair_update = jnp.dot(outer_mean, outer_mix, preferred_element_type=jnp.float32).reshape(block_rows, N, C)
        pair_block = lax.dynamic_slice_in_dim(pair_grid, first_row, block_rows, 0)
        return (pair_block.astype(jnp.float32) + pair_update).astype(jnp.bfloat16)
    pair_one = lax.map(outer_step, start_rows).reshape(N, N, C)
    pair_norm = normalize(pair_one, 2).astype(jnp.bfloat16)
    flat_norm = pair_norm.reshape(N * N, C)
    scores = jnp.dot(flat_norm, pair_logit, preferred_element_type=jnp.float32).reshape(N, N, H)
    weights = jnp.exp(scores)
    totals = lax.optimization_barrier(jnp.sum(weights, axis=1))
    column_values = jnp.dot(align_flat, average_proj[:, :H * HC], preferred_element_type=jnp.float32).astype(jnp.bfloat16).reshape(S, N, H, HC)
    gate_values = jax.nn.sigmoid(jnp.dot(align_flat, average_proj[:, H * HC:], preferred_element_type=jnp.float32)).reshape(S, N, H, HC)
    weighted = jnp.einsum('ijh,sjhc->sihc', settle_wide(weights.astype(jnp.bfloat16)), settle_wide(column_values))
    averaged = (gate_values * weighted / totals[None, :, :, None]).astype(jnp.bfloat16).reshape(S * N, H * HC)
    align_update = jnp.dot(averaged, average_mix, preferred_element_type=jnp.float32).reshape(S, N, CM)
    alignment_next = (alignments.astype(jnp.float32) + align_update).astype(jnp.bfloat16)
    mask_values = token_mask.astype(jnp.float32)
    pair_mask = mask_values[:, None] * mask_values[None, :]

    def channel_step(channel):
        picks = channel + C * jnp.arange(4, dtype=jnp.int32)
        columns = jnp.take(triangle_proj, picks, axis=1)
        projected = jnp.dot(flat_norm, columns, preferred_element_type=jnp.float32).reshape(N, N, 4)
        left_side = (jax.nn.sigmoid(projected[:, :, 0]) * projected[:, :, 1] * pair_mask).astype(jnp.bfloat16)
        right_side = (jax.nn.sigmoid(projected[:, :, 2]) * projected[:, :, 3] * pair_mask).astype(jnp.bfloat16)
        return jnp.dot(left_side, right_side.T, preferred_element_type=jnp.float32).astype(jnp.bfloat16)
    product = lax.map(channel_step, jnp.arange(C, dtype=jnp.int32))
    gate_weight = triangle_proj[:, 4 * C:]
    pair_rows_all = pair_one.reshape(N * N, C)

    def tail_step(first_row):
        product_block = lax.dynamic_slice_in_dim(product, first_row, block_rows, 1)
        product_norm = normalize(product_block, 0).astype(jnp.bfloat16).reshape(C, block_rows * N)
        mixed = lax.dot_general(product_norm, triangle_mix, (((0,), (0,)), ((), ())), preferred_element_type=jnp.float32)
        norm_rows = lax.dynamic_slice_in_dim(flat_norm, first_row * N, block_rows * N, 0)
        gate_out = jax.nn.sigmoid(jnp.dot(norm_rows, gate_weight, preferred_element_type=jnp.float32))
        pair_rows = lax.dynamic_slice_in_dim(pair_rows_all, first_row * N, block_rows * N, 0)
        pair_two = (pair_rows.astype(jnp.float32) + gate_out * mixed).astype(jnp.bfloat16)
        normed = normalize(pair_two, 1).astype(jnp.bfloat16)
        expanded = jnp.dot(normed, transition_up, preferred_element_type=jnp.float32)
        hidden = (jax.nn.silu(expanded[:, :TR]) * expanded[:, TR:]).astype(jnp.bfloat16)
        return (settle_wide(pair_two) + jnp.dot(hidden, transition_down, preferred_element_type=jnp.float32)).astype(jnp.bfloat16)
    pair_next = lax.map(tail_step, start_rows).reshape(N, N, C)
    return (pair_next, alignment_next)
```

```python
import functools

import jax
import jax.numpy as jnp
from jax import lax
from jax.experimental import pallas as pl
from jax.experimental.pallas import tpu as pltpu
from jax.sharding import PartitionSpec as P

epsilon = 1e-05


def normalize(values, channel_dim):
    values = values.astype(jnp.float32)
    centred = values - jnp.mean(values, axis=channel_dim, keepdims=True)
    spread = jnp.mean(centred * centred, axis=channel_dim, keepdims=True)
    return centred / jnp.sqrt(spread + epsilon)


def gather_kernel(n_row, n_col, block_ref, out_ref, own_sem, send_sems, far_sems, recv_sems):
    span = n_row // n_col
    row = lax.axis_index("row")
    col = lax.axis_index("col")
    band = row // span
    place = lax.rem(row, span)
    parity = lax.rem(place, 2)
    base = band * span
    twin_place = place + 1 - 2 * parity
    is_source = band == col
    half = span // 2

    def other_band(k):
        return lax.rem(band + k, n_col) * span + place

    def peer_place(k):
        return lax.rem(place + 2 * k, span)

    barrier = pltpu.get_barrier_semaphore()
    for k in range(1, n_col):
        pl.semaphore_signal(barrier, inc=1, device_id={"row": other_band(k)})
    pl.semaphore_signal(barrier, inc=1, device_id={"row": base + twin_place})
    for k in range(1, half):
        pl.semaphore_signal(barrier, inc=1, device_id={"row": base + peer_place(k)})
    pl.semaphore_wait(barrier, n_col - 1 + half)

    def push(source, slot, sem, recv, target):
        return pltpu.make_async_remote_copy(
            src_ref=source,
            dst_ref=out_ref.at[slot],
            send_sem=sem,
            recv_sem=recv,
            device_id={"row": target},
        )

    def far(k):
        return push(block_ref, place, far_sems.at[k - 1], recv_sems.at[place], other_band(k))

    @pl.when(is_source)
    def _():
        for k in range(1, n_col):
            far(k).start()
        own = pltpu.make_async_copy(block_ref, out_ref.at[place], own_sem)
        own.start()
        own.wait()

    @pl.when(jnp.logical_not(is_source))
    def _():
        push(block_ref, place, own_sem, recv_sems.at[place], base + twin_place).wait_recv()

    mine = out_ref.at[place]
    near = [
        push(mine, place, send_sems.at[k - 1], recv_sems.at[place], base + peer_place(k))
        for k in range(1, half)
    ]
    near.append(push(mine, place, send_sems.at[half - 1], recv_sems.at[place], base + twin_place))
    for copy in near:
        copy.start()
    for k in range(1, half):
        came = lax.rem(place - 2 * k + span, span)
        push(mine, came, own_sem, recv_sems.at[came], base + twin_place).wait_recv()
        onward = push(
            out_ref.at[came],
            came,
            send_sems.at[half - 1 + k],
            recv_sems.at[came],
            base + twin_place,
        )
        onward.start()
        near.append(onward)
    for k in range(half):
        came = lax.rem(twin_place + 2 * k, span)
        push(mine, came, own_sem, recv_sems.at[came], base + twin_place).wait_recv()
    for copy in near:
        copy.wait_send()

    @pl.when(is_source)
    def _():
        for k in range(1, n_col):
            far(k).wait_send()


def gather_blocks(block, collective_id):
    n_row = lax.axis_size("row")
    n_col = lax.axis_size("col")
    span = n_row // n_col
    return pl.pallas_call(
        functools.partial(gather_kernel, n_row, n_col),
        out_shape=jax.ShapeDtypeStruct((span,) + block.shape, block.dtype),
        in_specs=[pl.BlockSpec(memory_space=pltpu.VMEM)],
        out_specs=pl.BlockSpec(memory_space=pltpu.VMEM),
        scratch_shapes=[
            pltpu.SemaphoreType.DMA,
            pltpu.SemaphoreType.DMA((span,)),
            pltpu.SemaphoreType.DMA((max(n_col - 1, 1),)),
            pltpu.SemaphoreType.DMA((span,)),
        ],
        compiler_params=pltpu.CompilerParams(
            collective_id=collective_id, has_side_effects=True
        ),
        name=f"gather_{collective_id}",
    )(block)


def sum_columns(values, wire_dtype):
    n_col = lax.axis_size("col")
    total = values
    sent = values.astype(wire_dtype)
    for shift in range(1, n_col):
        pairs = [(k, (k + shift) % n_col) for k in range(n_col)]
        total = total + lax.ppermute(sent, "col", pairs).astype(jnp.float32)
    return total


def product_kernel(n_row, n_col, tok_row, tok_col, received_ref, out_ref, left_ref, right_ref):
    for r in range(n_row):
        for u in range(n_col):
            rows = slice(r * tok_row, (r + 1) * tok_row)
            lanes = slice(u * tok_col, (u + 1) * tok_col)
            left_ref[rows, lanes] = received_ref[0, r * n_col + u, 0]
            right_ref[rows, lanes] = received_ref[1, r * n_col + u, 0]
    result = lax.dot_general(
        left_ref[...], right_ref[...], (((1,), (1,)), ((), ())), preferred_element_type=jnp.float32
    ).astype(jnp.bfloat16)
    for r in range(n_row):
        for u in range(n_col):
            rows = slice(r * tok_row, (r + 1) * tok_row)
            lanes = slice(u * tok_col, (u + 1) * tok_col)
            out_ref[r * n_col + u, 0] = result[rows, lanes]


def triangle_product(received, n_row, n_col):
    _, devices, items, tok_row, tok_col = received.shape
    length = n_row * tok_row
    return pl.pallas_call(
        functools.partial(product_kernel, n_row, n_col, tok_row, tok_col),
        grid=(items,),
        out_shape=jax.ShapeDtypeStruct((devices, items, tok_row, tok_col), jnp.bfloat16),
        in_specs=[
            pl.BlockSpec((2, devices, 1, tok_row, tok_col), lambda c: (0, 0, c, 0, 0))
        ],
        out_specs=pl.BlockSpec((devices, 1, tok_row, tok_col), lambda c: (0, c, 0, 0)),
        scratch_shapes=[
            pltpu.VMEM((length, length), jnp.bfloat16),
            pltpu.VMEM((length, length), jnp.bfloat16),
        ],
        name="triangle_product",
    )(received)


def on_device(
    pair_grid,
    alignment_pool,
    sample_index,
    token_mask,
    outer_proj,
    outer_mix,
    pair_logit,
    average_proj,
    average_mix,
    triangle_proj,
    triangle_mix,
    transition_up,
    transition_down,
):
    n_row = lax.axis_size("row")
    n_col = lax.axis_size("col")
    tok_row = pair_grid.shape[0]
    tok_col = pair_grid.shape[1]
    pair_width = pair_grid.shape[2]
    samples = sample_index.shape[0]
    align_width = alignment_pool.shape[2]
    outer_width = outer_proj.shape[1] // 2
    head_count = pair_logit.shape[1]
    head_total = average_proj.shape[1] // 2
    head_dim = head_total // head_count
    inner_width = transition_down.shape[0]
    row_start = lax.axis_index("row") * tok_row
    column_start = lax.axis_index("col") * tok_col
    alignments = jnp.take(alignment_pool, sample_index, axis=0)
    align_norm = normalize(alignments, 2).astype(jnp.bfloat16)
    align_rows = align_norm.reshape(samples, tok_row * align_width)
    gathered = gather_blocks(align_rows, 0)
    column_norm = (
        gathered.reshape(n_row // n_col, samples, tok_row, align_width)
        .transpose(1, 0, 2, 3)
        .reshape(samples, tok_col, align_width)
    )
    row_factor = jnp.dot(
        align_norm, outer_proj[:, :outer_width], preferred_element_type=jnp.float32
    ).astype(jnp.bfloat16)
    column_factor = jnp.dot(
        column_norm, outer_proj[:, outer_width:], preferred_element_type=jnp.float32
    ).astype(jnp.bfloat16)
    column_rows = column_factor.reshape(samples, tok_col * outer_width)
    block_rows = 8
    block_count = tok_row // block_rows
    row_blocks = row_factor.reshape(samples, block_count, block_rows * outer_width).transpose(
        1, 0, 2
    )
    pair_blocks = pair_grid.reshape(block_count, block_rows, tok_col, pair_width)

    def outer_step(operands):
        left_block, pair_block = operands
        outer_sum = lax.dot_general(
            left_block, column_rows, (((0,), (0,)), ((), ())), preferred_element_type=jnp.float32
        )
        outer_sum = outer_sum.reshape(block_rows, outer_width, tok_col, outer_width).transpose(
            0, 2, 1, 3
        )
        outer_mean = (
            (outer_sum * (1.0 / samples))
            .astype(jnp.bfloat16)
            .reshape(block_rows * tok_col, outer_width * outer_width)
        )
        update = jnp.dot(outer_mean, outer_mix, preferred_element_type=jnp.float32).reshape(
            block_rows, tok_col, pair_width
        )
        return (pair_block.astype(jnp.float32) + update).astype(jnp.bfloat16)

    pair_one = lax.map(outer_step, (row_blocks, pair_blocks)).reshape(tok_row, tok_col, pair_width)
    pair_norm = normalize(pair_one, 2).astype(jnp.bfloat16)
    value_weight = average_proj[:, :head_total].reshape(align_width, head_count, head_dim)
    gate_weight = average_proj[:, head_total:].reshape(align_width, head_count, head_dim)
    mix_weight = average_mix.reshape(head_count, head_dim, align_width)
    scores = lax.dot_general(
        pair_logit, pair_norm, (((0,), (2,)), ((), ())), preferred_element_type=jnp.float32
    )
    weights = jnp.exp(scores)
    partial_total = jnp.sum(weights, axis=2)
    weights_low = weights.astype(jnp.bfloat16)
    column_values = jnp.einsum(
        "sjm,mhc->hjsc", column_norm, value_weight, preferred_element_type=jnp.float32
    )
    column_values = column_values.astype(jnp.bfloat16).reshape(
        head_count, tok_col, samples * head_dim
    )
    partial_sum = jnp.einsum(
        "hij,hjk->hik", weights_low, column_values, preferred_element_type=jnp.float32
    )
    weighted = sum_columns(partial_sum, jnp.bfloat16)
    totals = sum_columns(partial_total, jnp.float32)
    gate_values = jax.nn.sigmoid(
        jnp.einsum("sim,mhc->hisc", align_norm, gate_weight, preferred_element_type=jnp.float32)
    )
    weighted = weighted.reshape(head_count, tok_row, samples, head_dim)
    averaged = (gate_values * weighted / totals[:, :, None, None]).astype(jnp.bfloat16)
    align_update = jnp.einsum(
        "hisc,hcm->sim", averaged, mix_weight, preferred_element_type=jnp.float32
    )
    alignment_next = (alignments.astype(jnp.float32) + align_update).astype(jnp.bfloat16)
    flat_norm = pair_norm.reshape(tok_row * tok_col, pair_width)
    projected = lax.dot_general(
        triangle_proj[:, : 4 * pair_width],
        flat_norm,
        (((0,), (1,)), ((), ())),
        preferred_element_type=jnp.float32,
    )
    projected = projected.reshape(4, pair_width, tok_row, tok_col)
    row_mask = lax.dynamic_slice_in_dim(token_mask, row_start, tok_row, 0).astype(jnp.float32)
    column_mask = lax.dynamic_slice_in_dim(token_mask, column_start, tok_col, 0).astype(jnp.float32)
    pair_mask = row_mask[:, None] * column_mask[None, :]
    left_side = jax.nn.sigmoid(projected[0]) * projected[1] * pair_mask
    right_side = jax.nn.sigmoid(projected[2]) * projected[3] * pair_mask
    factors = jnp.stack([left_side, right_side]).astype(jnp.bfloat16)
    group_size = pair_width // (n_row * n_col)
    grouped = factors.reshape(2, n_row * n_col, group_size, tok_row, tok_col)
    received = lax.all_to_all(grouped, ("row", "col"), split_axis=1, concat_axis=1, tiled=True)
    flat_result = triangle_product(received, n_row, n_col)
    product = lax.all_to_all(flat_result, ("row", "col"), split_axis=0, concat_axis=0, tiled=True)
    product = product.reshape(pair_width, tok_row, tok_col)
    product_norm = normalize(product, 0).astype(jnp.bfloat16).reshape(pair_width, tok_row * tok_col)
    mixed = lax.dot_general(
        product_norm, triangle_mix, (((0,), (0,)), ((), ())), preferred_element_type=jnp.float32
    )
    gate_out = jax.nn.sigmoid(
        jnp.dot(flat_norm, triangle_proj[:, 4 * pair_width :], preferred_element_type=jnp.float32)
    )
    pair_two = (
        pair_one.reshape(tok_row * tok_col, pair_width).astype(jnp.float32) + gate_out * mixed
    ).astype(jnp.bfloat16)
    tail_rows = pair_two.reshape(block_count, block_rows * tok_col, pair_width)

    def transition_step(rows_block):
        normed = normalize(rows_block, 1).astype(jnp.bfloat16)
        expanded = jnp.dot(normed, transition_up, preferred_element_type=jnp.float32)
        hidden = (jax.nn.silu(expanded[:, :inner_width]) * expanded[:, inner_width:]).astype(
            jnp.bfloat16
        )
        return (
            rows_block.astype(jnp.float32)
            + jnp.dot(hidden, transition_down, preferred_element_type=jnp.float32)
        ).astype(jnp.bfloat16)

    pair_next = lax.map(transition_step, tail_rows).reshape(tok_row, tok_col, pair_width)
    return (pair_next, alignment_next)


def solution(mesh):
    in_specs = (
        P(("groups", "row"), "col", None),
        P("groups", "row", None),
        P("groups"),
        P("groups"),
        P(),
        P(),
        P(),
        P(),
        P(),
        P(),
        P(),
        P(),
        P(),
    )
    out_specs = (P(("groups", "row"), "col", None), P("groups", "row", None))
    return jax.shard_map(
        on_device, mesh=mesh, in_specs=in_specs, out_specs=out_specs, check_vma=False
    )
```

```python
import functools

import jax
import jax.numpy as jnp
from jax import lax
from jax.experimental import pallas as pl
from jax.experimental.pallas import tpu as pltpu
from jax.sharding import PartitionSpec as P

epsilon = 1e-05


def normalize(values, channel_dim):
    values = values.astype(jnp.float32)
    centred = values - jnp.mean(values, axis=channel_dim, keepdims=True)
    spread = jnp.mean(centred * centred, axis=channel_dim, keepdims=True)
    return centred / jnp.sqrt(spread + epsilon)


def gather_kernel(n_row, n_col, block_ref, out_ref, own_sem, send_sems, far_sems, recv_sems):
    span = n_row // n_col
    row = lax.axis_index("row")
    col = lax.axis_index("col")
    band = row // span
    place = lax.rem(row, span)
    parity = lax.rem(place, 2)
    base = band * span
    twin_place = place + 1 - 2 * parity
    is_source = band == col
    half = span // 2

    def other_band(k):
        return lax.rem(band + k, n_col) * span + place

    def peer_place(k):
        return lax.rem(place + 2 * k, span)

    barrier = pltpu.get_barrier_semaphore()
    for k in range(1, n_col):
        pl.semaphore_signal(barrier, inc=1, device_id={"row": other_band(k)})
    pl.semaphore_signal(barrier, inc=1, device_id={"row": base + twin_place})
    for k in range(1, half):
        pl.semaphore_signal(barrier, inc=1, device_id={"row": base + peer_place(k)})
    pl.semaphore_wait(barrier, n_col - 1 + half)

    def push(source, slot, sem, recv, target):
        return pltpu.make_async_remote_copy(
            src_ref=source,
            dst_ref=out_ref.at[slot],
            send_sem=sem,
            recv_sem=recv,
            device_id={"row": target},
        )

    def far(k):
        return push(block_ref, place, far_sems.at[k - 1], recv_sems.at[place], other_band(k))

    @pl.when(is_source)
    def _():
        for k in range(1, n_col):
            far(k).start()
        own = pltpu.make_async_copy(block_ref, out_ref.at[place], own_sem)
        own.start()
        own.wait()

    @pl.when(jnp.logical_not(is_source))
    def _():
        push(block_ref, place, own_sem, recv_sems.at[place], base + twin_place).wait_recv()

    mine = out_ref.at[place]
    near = [
        push(mine, place, send_sems.at[k - 1], recv_sems.at[place], base + peer_place(k))
        for k in range(1, half)
    ]
    near.append(push(mine, place, send_sems.at[half - 1], recv_sems.at[place], base + twin_place))
    for copy in near:
        copy.start()
    for k in range(1, half):
        came = lax.rem(place - 2 * k + span, span)
        push(mine, came, own_sem, recv_sems.at[came], base + twin_place).wait_recv()
        onward = push(
            out_ref.at[came],
            came,
            send_sems.at[half - 1 + k],
            recv_sems.at[came],
            base + twin_place,
        )
        onward.start()
        near.append(onward)
    for k in range(half):
        came = lax.rem(twin_place + 2 * k, span)
        push(mine, came, own_sem, recv_sems.at[came], base + twin_place).wait_recv()
    for copy in near:
        copy.wait_send()

    @pl.when(is_source)
    def _():
        for k in range(1, n_col):
            far(k).wait_send()


def gather_blocks(block, collective_id):
    n_row = lax.axis_size("row")
    n_col = lax.axis_size("col")
    span = n_row // n_col
    return pl.pallas_call(
        functools.partial(gather_kernel, n_row, n_col),
        out_shape=jax.ShapeDtypeStruct((span,) + block.shape, block.dtype),
        in_specs=[pl.BlockSpec(memory_space=pltpu.VMEM)],
        out_specs=pl.BlockSpec(memory_space=pltpu.VMEM),
        scratch_shapes=[
            pltpu.SemaphoreType.DMA,
            pltpu.SemaphoreType.DMA((span,)),
            pltpu.SemaphoreType.DMA((max(n_col - 1, 1),)),
            pltpu.SemaphoreType.DMA((span,)),
        ],
        compiler_params=pltpu.CompilerParams(
            collective_id=collective_id, has_side_effects=True
        ),
        name=f"gather_{collective_id}",
    )(block)


def sum_columns(values, wire_dtype):
    n_col = lax.axis_size("col")
    total = values
    sent = values.astype(wire_dtype)
    for shift in range(1, n_col):
        pairs = [(k, (k + shift) % n_col) for k in range(n_col)]
        total = total + lax.ppermute(sent, "col", pairs).astype(jnp.float32)
    return total


def product_kernel(n_row, n_col, tok_row, tok_col, received_ref, out_ref, left_ref, right_ref):
    for r in range(n_row):
        for u in range(n_col):
            rows = slice(r * tok_row, (r + 1) * tok_row)
            lanes = slice(u * tok_col, (u + 1) * tok_col)
            left_ref[rows, lanes] = received_ref[r * n_col + u, 0, 0]
            right_ref[rows, lanes] = received_ref[r * n_col + u, 1, 0]
    result = lax.dot_general(
        left_ref[...], right_ref[...], (((1,), (1,)), ((), ())), preferred_element_type=jnp.float32
    ).astype(jnp.bfloat16)
    for r in range(n_row):
        for u in range(n_col):
            rows = slice(r * tok_row, (r + 1) * tok_row)
            lanes = slice(u * tok_col, (u + 1) * tok_col)
            out_ref[r * n_col + u, 0] = result[rows, lanes]


def triangle_product(received, n_row, n_col):
    devices, _, items, tok_row, tok_col = received.shape
    length = n_row * tok_row
    return pl.pallas_call(
        functools.partial(product_kernel, n_row, n_col, tok_row, tok_col),
        grid=(items,),
        out_shape=jax.ShapeDtypeStruct((devices, items, tok_row, tok_col), jnp.bfloat16),
        in_specs=[
            pl.BlockSpec((devices, 2, 1, tok_row, tok_col), lambda c: (0, 0, c, 0, 0))
        ],
        out_specs=pl.BlockSpec((devices, 1, tok_row, tok_col), lambda c: (0, c, 0, 0)),
        scratch_shapes=[
            pltpu.VMEM((length, length), jnp.bfloat16),
            pltpu.VMEM((length, length), jnp.bfloat16),
        ],
        name="triangle_product",
    )(received)


def prep_kernel(
    index_ref, pool_ref, row_weight_ref, column_weight_ref, align_ref, norm_ref, row_ref, column_ref, held_ref
):
    tok_row, align_width, stored = pool_ref.shape
    samples = align_ref.shape[1]
    outer_width = row_weight_ref.shape[1]
    half = outer_width // 2
    slots = lax.broadcasted_iota(jnp.int32, (2 * samples, stored), 1)
    picks = (slots == index_ref[...]).astype(jnp.bfloat16)
    lanes = lax.broadcasted_iota(jnp.int32, (half, 2 * samples), 1)
    for t in range(tok_row):
        twice = lax.dot_general(
            picks, pool_ref[t], (((1,), (1,)), ((), ())), preferred_element_type=jnp.float32
        )
        normed = normalize(twice, 1).astype(jnp.bfloat16)
        align_ref[t] = twice[:samples].astype(jnp.bfloat16)
        norm_ref[t] = normed[:samples]
        row_ref[t * samples : (t + 1) * samples, :] = jnp.dot(
            normed[:samples], row_weight_ref[...], preferred_element_type=jnp.float32
        ).astype(jnp.bfloat16)
        factor = lax.dot_general(
            column_weight_ref[...],
            normed,
            (((1,), (1,)), ((), ())),
            preferred_element_type=jnp.float32,
        )
        held_ref[t * half : (t + 1) * half, :] = jnp.where(
            lanes < samples, factor[:half], factor[half:]
        )
    for d in range(half):
        column_ref[:, d * 2 * samples : (d + 1) * 2 * samples] = held_ref[
            pl.ds(d, tok_row, stride=half), :
        ].astype(jnp.bfloat16)


def prepare(alignment_pool, sample_index, outer_proj):
    stored, tok_row, align_width = alignment_pool.shape
    samples = sample_index.shape[0]
    outer_width = outer_proj.shape[1] // 2
    half = outer_width // 2
    spread = jnp.concatenate([sample_index, sample_index])[:, None]
    return pl.pallas_call(
        prep_kernel,
        out_shape=(
            jax.ShapeDtypeStruct((tok_row, samples, align_width), jnp.bfloat16),
            jax.ShapeDtypeStruct((tok_row, samples, align_width), jnp.bfloat16),
            jax.ShapeDtypeStruct((tok_row * samples, outer_width), jnp.bfloat16),
            jax.ShapeDtypeStruct((tok_row, outer_width * samples), jnp.bfloat16),
        ),
        scratch_shapes=[pltpu.VMEM((tok_row * half, 2 * samples), jnp.float32)],
        name="prepare",
    )(
        spread,
        alignment_pool.transpose(1, 2, 0),
        outer_proj[:, :outer_width],
        outer_proj[:, outer_width:].T,
    )


def pair_kernel(
    steps,
    step_rows,
    samples,
    head_count,
    column_ref,
    row_ref,
    mix_ref,
    grid_ref,
    weight_ref,
    mask_ref,
    one_ref,
    norm_ref,
    score_ref,
    factor_ref,
    held_ref,
):
    step = pl.program_id(0)
    pair_width = grid_ref.shape[2]
    outer_width = row_ref.shape[1]
    half = outer_width // 2
    tok_row = steps * step_rows
    order = [side * half + d for d in range(half) for side in range(2)]
    spread = jnp.dot(row_ref[...], mix_ref[...], preferred_element_type=jnp.float32).astype(
        jnp.bfloat16
    )
    for k in range(step_rows):
        piece = spread[k * samples : (k + 1) * samples]
        stacked = jnp.concatenate(
            [piece[:, d * pair_width : (d + 1) * pair_width] for d in order], axis=0
        )
        update = jnp.dot(column_ref[...], stacked, preferred_element_type=jnp.float32)
        pair_one = (grid_ref[k].astype(jnp.float32) + update * (1.0 / samples)).astype(jnp.bfloat16)
        one_ref[k] = pair_one
        pair_norm = normalize(pair_one, 1).astype(jnp.bfloat16)
        norm_ref[k] = pair_norm
        projected = lax.dot_general(
            weight_ref[...],
            pair_norm,
            (((1,), (1,)), ((), ())),
            preferred_element_type=jnp.float32,
        )
        mask = mask_ref[k]
        row = step * step_rows + k
        for side in range(2):
            base = 2 * side * pair_width
            gate = projected[base : base + pair_width]
            value = projected[base + pair_width : base + 2 * pair_width]
            held_ref[side, pl.ds(row, pair_width, stride=tok_row), :] = (
                jax.nn.sigmoid(gate) * value * mask
            )
        score_ref[k] = jnp.exp(projected[4 * pair_width : 4 * pair_width + head_count])

    @pl.when(step == steps - 1)
    def _():
        devices, _, group, _, tok_col = factor_ref.shape
        for side in range(2):
            factor_ref[:, side] = (
                held_ref[side].astype(jnp.bfloat16).reshape(devices, group, tok_row, tok_col)
            )


def pair_stage(columns, rows, outer_mix, pair_grid, triangle_proj, pair_logit, pair_mask, devices):
    tok_row, tok_col, pair_width = pair_grid.shape
    outer_width = rows.shape[1]
    samples = rows.shape[0] // tok_row
    head_count = pair_logit.shape[1]
    step_rows = 2 if tok_row % 2 == 0 else 1
    steps = tok_row // step_rows
    group = pair_width // devices
    mix = outer_mix.reshape(outer_width, outer_width * pair_width)
    weights = jnp.concatenate([triangle_proj[:, : 4 * pair_width], pair_logit], axis=1).T
    whole = lambda *shape: pl.BlockSpec(shape, lambda r: (0,) * len(shape))
    part = lambda *shape: pl.BlockSpec(shape, lambda r: (r,) + (0,) * (len(shape) - 1))
    return pl.pallas_call(
        functools.partial(pair_kernel, steps, step_rows, samples, head_count),
        grid=(steps,),
        out_shape=(
            jax.ShapeDtypeStruct(pair_grid.shape, jnp.bfloat16),
            jax.ShapeDtypeStruct(pair_grid.shape, jnp.bfloat16),
            jax.ShapeDtypeStruct((tok_row, head_count, tok_col), jnp.float32),
            jax.ShapeDtypeStruct((devices, 2, group, tok_row, tok_col), jnp.bfloat16),
        ),
        in_specs=[
            whole(*columns.shape),
            part(step_rows * samples, outer_width),
            whole(*mix.shape),
            part(step_rows, tok_col, pair_width),
            whole(*weights.shape),
            part(step_rows, 1, tok_col),
        ],
        out_specs=(
            part(step_rows, tok_col, pair_width),
            part(step_rows, tok_col, pair_width),
            part(step_rows, head_count, tok_col),
            whole(devices, 2, group, tok_row, tok_col),
        ),
        scratch_shapes=[pltpu.VMEM((2, pair_width * tok_row, tok_col), jnp.float32)],
        name="pair_stage",
    )(columns, rows, mix, pair_grid, weights, pair_mask[:, None, :])


def tail_kernel(
    step_rows, product_ref, one_ref, gate_ref, mix_ref, up_ref, down_ref, out_ref, held_ref
):
    step = pl.program_id(0)
    devices, group, tok_row, tok_col = product_ref.shape
    pair_width = devices * group
    inner_width = down_ref.shape[0]

    @pl.when(step == 0)
    def _():
        held_ref[...] = (
            product_ref[...].astype(jnp.float32).reshape(pair_width * tok_row, tok_col)
        )

    rows = []
    for k in range(step_rows):
        product = held_ref[pl.ds(step * step_rows + k, pair_width, stride=tok_row), :]
        normed = normalize(product, 0).astype(jnp.bfloat16)
        mixed = lax.dot_general(
            normed, mix_ref[...], (((0,), (0,)), ((), ())), preferred_element_type=jnp.float32
        )
        rows.append((one_ref[k].astype(jnp.float32) + gate_ref[k] * mixed).astype(jnp.bfloat16))
    pair_two = jnp.concatenate(rows, axis=0)
    normed = normalize(pair_two, 1).astype(jnp.bfloat16)
    expanded = jnp.dot(normed, up_ref[...], preferred_element_type=jnp.float32)
    hidden = (jax.nn.silu(expanded[:, :inner_width]) * expanded[:, inner_width:]).astype(
        jnp.bfloat16
    )
    result = (
        pair_two.astype(jnp.float32)
        + jnp.dot(hidden, down_ref[...], preferred_element_type=jnp.float32)
    ).astype(jnp.bfloat16)
    for k in range(step_rows):
        out_ref[k] = result[k * tok_col : (k + 1) * tok_col]


def tail_stage(product, pair_one, gate_out, triangle_mix, transition_up, transition_down):
    tok_row, tok_col, pair_width = pair_one.shape
    step_rows = 2 if tok_row % 2 == 0 else 1
    whole = lambda *shape: pl.BlockSpec(shape, lambda r: (0,) * len(shape))
    part = lambda *shape: pl.BlockSpec(shape, lambda r: (r,) + (0,) * (len(shape) - 1))
    block = part(step_rows, tok_col, pair_width)
    return pl.pallas_call(
        functools.partial(tail_kernel, step_rows),
        grid=(tok_row // step_rows,),
        out_shape=jax.ShapeDtypeStruct(pair_one.shape, jnp.bfloat16),
        in_specs=[
            whole(*product.shape),
            block,
            block,
            whole(*triangle_mix.shape),
            whole(*transition_up.shape),
            whole(*transition_down.shape),
        ],
        out_specs=block,
        scratch_shapes=[pltpu.VMEM((pair_width * tok_row, tok_col), jnp.float32)],
        name="tail_stage",
    )(product, pair_one, gate_out, triangle_mix, transition_up, transition_down)


def on_device(
    pair_grid,
    alignment_pool,
    sample_index,
    token_mask,
    outer_proj,
    outer_mix,
    pair_logit,
    average_proj,
    average_mix,
    triangle_proj,
    triangle_mix,
    transition_up,
    transition_down,
):
    n_row = lax.axis_size("row")
    n_col = lax.axis_size("col")
    tok_row = pair_grid.shape[0]
    tok_col = pair_grid.shape[1]
    pair_width = pair_grid.shape[2]
    samples = sample_index.shape[0]
    align_width = alignment_pool.shape[2]
    head_count = pair_logit.shape[1]
    head_total = average_proj.shape[1] // 2
    head_dim = head_total // head_count
    row_start = lax.axis_index("row") * tok_row
    column_start = lax.axis_index("col") * tok_col
    row_mask = lax.dynamic_slice_in_dim(token_mask, row_start, tok_row, 0).astype(jnp.float32)
    column_mask = lax.dynamic_slice_in_dim(token_mask, column_start, tok_col, 0).astype(jnp.float32)
    pair_mask = row_mask[:, None] * column_mask[None, :]
    alignments, align_norm, rows, column_block = prepare(alignment_pool, sample_index, outer_proj)
    columns = gather_blocks(column_block, 0).reshape(tok_col, column_block.shape[1])
    pair_one, pair_norm, weights, factors = pair_stage(
        columns,
        rows,
        outer_mix,
        pair_grid,
        triangle_proj,
        pair_logit,
        pair_mask,
        n_row * n_col,
    )
    received = lax.all_to_all(factors, ("row", "col"), split_axis=0, concat_axis=0, tiled=True)
    align_rows = align_norm.transpose(1, 0, 2).reshape(samples, tok_row * align_width)
    align_rows, weights = lax.optimization_barrier((align_rows, weights))
    gathered = gather_blocks(align_rows, 1)
    column_norm = (
        gathered.reshape(n_row // n_col, samples, tok_row, align_width)
        .transpose(1, 0, 2, 3)
        .reshape(samples, tok_col, align_width)
    )
    value_weight = average_proj[:, :head_total].reshape(align_width, head_count, head_dim)
    gate_weight = average_proj[:, head_total:].reshape(align_width, head_count, head_dim)
    mix_weight = average_mix.reshape(head_count, head_dim, align_width)
    weights = weights.transpose(1, 0, 2)
    partial_total = jnp.sum(weights, axis=2)
    weights_low = weights.astype(jnp.bfloat16)
    column_values = jnp.einsum(
        "sjm,mhc->hjsc", column_norm, value_weight, preferred_element_type=jnp.float32
    )
    column_values = column_values.astype(jnp.bfloat16).reshape(
        head_count, tok_col, samples * head_dim
    )
    partial_sum = jnp.einsum(
        "hij,hjk->hik", weights_low, column_values, preferred_element_type=jnp.float32
    )
    weighted = sum_columns(partial_sum, jnp.bfloat16)
    totals = sum_columns(partial_total, jnp.float32)
    gate_values = jax.nn.sigmoid(
        jnp.einsum("ism,mhc->hisc", align_norm, gate_weight, preferred_element_type=jnp.float32)
    )
    weighted = weighted.reshape(head_count, tok_row, samples, head_dim)
    averaged = (gate_values * weighted / totals[:, :, None, None]).astype(jnp.bfloat16)
    align_update = jnp.einsum(
        "hisc,hcm->sim", averaged, mix_weight, preferred_element_type=jnp.float32
    )
    alignment_next = (
        alignments.transpose(1, 0, 2).astype(jnp.float32) + align_update
    ).astype(jnp.bfloat16)
    flat_result = triangle_product(received, n_row, n_col)
    product = lax.all_to_all(flat_result, ("row", "col"), split_axis=0, concat_axis=0, tiled=True)
    gate_out = jax.nn.sigmoid(
        jnp.dot(pair_norm, triangle_proj[:, 4 * pair_width :], preferred_element_type=jnp.float32)
    )
    pair_next = tail_stage(
        product, pair_one, gate_out, triangle_mix, transition_up, transition_down
    )
    return (pair_next, alignment_next)


def solution(mesh):
    in_specs = (
        P(("groups", "row"), "col", None),
        P("groups", "row", None),
        P("groups"),
        P("groups"),
        P(),
        P(),
        P(),
        P(),
        P(),
        P(),
        P(),
        P(),
        P(),
    )
    out_specs = (P(("groups", "row"), "col", None), P("groups", "row", None))
    return jax.shard_map(
        on_device, mesh=mesh, in_specs=in_specs, out_specs=out_specs, check_vma=False
    )
```

```python
import functools

import jax
import jax.numpy as jnp
from jax import lax
from jax.experimental import pallas as pl
from jax.experimental.pallas import tpu as pltpu
from jax.sharding import PartitionSpec as P

epsilon = 1e-05


def normalize(values, channel_dim):
    values = values.astype(jnp.float32)
    centred = values - jnp.mean(values, axis=channel_dim, keepdims=True)
    spread = jnp.mean(centred * centred, axis=channel_dim, keepdims=True)
    return centred * lax.rsqrt(spread + epsilon)


def gather_kernel(n_row, n_col, count, *refs):
    blocks, outs = refs[:count], refs[count : 2 * count]
    own_sem, send_sems, far_sems, recv_sems = refs[2 * count :]
    span = n_row // n_col
    row = lax.axis_index("row")
    col = lax.axis_index("col")
    band = row // span
    place = lax.rem(row, span)
    parity = lax.rem(place, 2)
    base = band * span
    twin_place = place + 1 - 2 * parity
    is_source = band == col
    half = span // 2

    def other_band(k):
        return lax.rem(band + k, n_col) * span + place

    def peer_place(k):
        return lax.rem(place + 2 * k, span)

    barrier = pltpu.get_barrier_semaphore()
    for k in range(1, n_col):
        pl.semaphore_signal(barrier, inc=1, device_id={"row": other_band(k)})
    pl.semaphore_signal(barrier, inc=1, device_id={"row": base + twin_place})
    for k in range(1, half):
        pl.semaphore_signal(barrier, inc=1, device_id={"row": base + peer_place(k)})
    pl.semaphore_wait(barrier, n_col - 1 + half)

    def push(n, source, slot, sem, target):
        return pltpu.make_async_remote_copy(
            src_ref=source,
            dst_ref=outs[n].at[slot],
            send_sem=sem,
            recv_sem=recv_sems.at[n, slot],
            device_id={"row": target},
        )

    def far(n, k):
        return push(n, blocks[n], place, far_sems.at[n, k - 1], other_band(k))

    def own_copy(n):
        return pltpu.make_async_copy(blocks[n], outs[n].at[place], own_sem.at[n])

    def arrival(n, slot):
        return push(n, outs[n].at[place], slot, own_sem.at[n], base + twin_place)

    @pl.when(is_source)
    def _():
        for n in range(count):
            for k in range(1, n_col):
                far(n, k).start()
            own_copy(n).start()
        for n in range(count):
            own_copy(n).wait()

    sent = []
    for n in range(count):

        @pl.when(jnp.logical_not(is_source))
        def _():
            arrival(n, place).wait_recv()

        mine = outs[n].at[place]
        near = [
            push(n, mine, place, send_sems.at[n, k - 1], base + peer_place(k))
            for k in range(1, half)
        ]
        near.append(push(n, mine, place, send_sems.at[n, half - 1], base + twin_place))
        for copy in near:
            copy.start()
        sent += near
    for n in range(count):
        for k in range(1, half):
            came = lax.rem(place - 2 * k + span, span)
            arrival(n, came).wait_recv()
            onward = push(
                n, outs[n].at[came], came, send_sems.at[n, half - 1 + k], base + twin_place
            )
            onward.start()
            sent.append(onward)
    for n in range(count):
        for k in range(half):
            arrival(n, lax.rem(twin_place + 2 * k, span)).wait_recv()
    for copy in sent:
        copy.wait_send()

    @pl.when(is_source)
    def _():
        for n in range(count):
            for k in range(1, n_col):
                far(n, k).wait_send()


def gather_blocks(*blocks):
    n_row = lax.axis_size("row")
    n_col = lax.axis_size("col")
    span = n_row // n_col
    count = len(blocks)
    return pl.pallas_call(
        functools.partial(gather_kernel, n_row, n_col, count),
        out_shape=tuple(
            jax.ShapeDtypeStruct((span,) + block.shape, block.dtype) for block in blocks
        ),
        in_specs=[pl.BlockSpec(memory_space=pltpu.VMEM)] * count,
        out_specs=tuple(pl.BlockSpec(memory_space=pltpu.VMEM) for _ in blocks),
        scratch_shapes=[
            pltpu.SemaphoreType.DMA((count,)),
            pltpu.SemaphoreType.DMA((count, span)),
            pltpu.SemaphoreType.DMA((count, max(n_col - 1, 1))),
            pltpu.SemaphoreType.DMA((count, span)),
        ],
        compiler_params=pltpu.CompilerParams(collective_id=0, has_side_effects=True),
        name="gather_blocks",
    )(*blocks)


def sum_columns(values, wire_dtype):
    n_col = lax.axis_size("col")
    total = values
    sent = values.astype(wire_dtype)
    for shift in range(1, n_col):
        pairs = [(k, (k + shift) % n_col) for k in range(n_col)]
        total = total + lax.ppermute(sent, "col", pairs).astype(jnp.float32)
    return total


def product_kernel(n_row, n_col, tok_row, tok_col, received_ref, out_ref, left_ref, right_ref):
    for r in range(n_row):
        for u in range(n_col):
            rows = slice(r * tok_row, (r + 1) * tok_row)
            lanes = slice(u * tok_col, (u + 1) * tok_col)
            left_ref[rows, lanes] = received_ref[r * n_col + u, 0, 0]
            right_ref[rows, lanes] = received_ref[r * n_col + u, 1, 0]
    result = lax.dot_general(
        left_ref[...], right_ref[...], (((1,), (1,)), ((), ())), preferred_element_type=jnp.float32
    ).astype(jnp.bfloat16)
    for r in range(n_row):
        for u in range(n_col):
            rows = slice(r * tok_row, (r + 1) * tok_row)
            lanes = slice(u * tok_col, (u + 1) * tok_col)
            out_ref[r * n_col + u, 0] = result[rows, lanes]


def triangle_product(received, n_row, n_col):
    devices, _, items, tok_row, tok_col = received.shape
    length = n_row * tok_row
    return pl.pallas_call(
        functools.partial(product_kernel, n_row, n_col, tok_row, tok_col),
        grid=(items,),
        out_shape=jax.ShapeDtypeStruct((devices, items, tok_row, tok_col), jnp.bfloat16),
        in_specs=[
            pl.BlockSpec((devices, 2, 1, tok_row, tok_col), lambda c: (0, 0, c, 0, 0))
        ],
        out_specs=pl.BlockSpec((devices, 1, tok_row, tok_col), lambda c: (0, c, 0, 0)),
        scratch_shapes=[
            pltpu.VMEM((length, length), jnp.bfloat16),
            pltpu.VMEM((length, length), jnp.bfloat16),
        ],
        name="triangle_product",
    )(received)


def prep_kernel(
    index_ref, pool_ref, proj_ref, align_ref, norm_ref, row_ref, column_ref, held_ref
):
    tok_row, align_width, stored = pool_ref.shape
    samples = align_ref.shape[1]
    outer_width = proj_ref.shape[1] // 2
    half = outer_width // 2
    slots = lax.broadcasted_iota(jnp.int32, (stored, samples), 0)
    picks = (slots == index_ref[...]).astype(jnp.float32).T.astype(jnp.bfloat16)
    lanes = lax.broadcasted_iota(jnp.int32, (half, 2 * samples), 1)
    row_weight = proj_ref[:, :outer_width]
    column_weight = proj_ref[...].astype(jnp.float32).T[outer_width:].astype(jnp.bfloat16)
    for t in range(tok_row):
        chosen = lax.dot_general(
            picks, pool_ref[t], (((1,), (1,)), ((), ())), preferred_element_type=jnp.float32
        )
        normed = normalize(chosen, 1).astype(jnp.bfloat16)
        align_ref[t] = chosen.astype(jnp.bfloat16)
        norm_ref[t] = normed
        row_ref[t * samples : (t + 1) * samples, :] = jnp.dot(
            normed, row_weight, preferred_element_type=jnp.float32
        ).astype(jnp.bfloat16)
        factor = lax.dot_general(
            column_weight,
            jnp.concatenate([normed, normed], axis=0),
            (((1,), (1,)), ((), ())),
            preferred_element_type=jnp.float32,
        )
        held_ref[t * half : (t + 1) * half, :] = jnp.where(
            lanes < samples, factor[:half], factor[half:]
        )
    for d in range(half):
        column_ref[:, d * 2 * samples : (d + 1) * 2 * samples] = held_ref[
            pl.ds(d, tok_row, stride=half), :
        ].astype(jnp.bfloat16)


def prepare(alignment_pool, sample_index, outer_proj):
    stored, tok_row, align_width = alignment_pool.shape
    samples = sample_index.shape[0]
    outer_width = outer_proj.shape[1] // 2
    half = outer_width // 2
    return pl.pallas_call(
        prep_kernel,
        out_shape=(
            jax.ShapeDtypeStruct((tok_row, samples, align_width), jnp.bfloat16),
            jax.ShapeDtypeStruct((tok_row, samples, align_width), jnp.bfloat16),
            jax.ShapeDtypeStruct((tok_row * samples, outer_width), jnp.bfloat16),
            jax.ShapeDtypeStruct((tok_row, outer_width * samples), jnp.bfloat16),
        ),
        scratch_shapes=[pltpu.VMEM((tok_row * half, 2 * samples), jnp.float32)],
        name="prepare",
    )(sample_index[None, :], alignment_pool.transpose(1, 2, 0), outer_proj)


def pair_kernel(
    steps,
    step_rows,
    samples,
    head_count,
    column_ref,
    row_ref,
    mix_ref,
    grid_ref,
    proj_ref,
    logit_ref,
    mask_ref,
    one_ref,
    norm_ref,
    score_ref,
    factor_ref,
    held_ref,
    wide_ref,
    mixed_ref,
    weight_ref,
):
    step = pl.program_id(0)
    pair_width = grid_ref.shape[2]
    outer_width = row_ref.shape[1]
    half = outer_width // 2
    tok_row = steps * step_rows
    order = [side * half + d for d in range(half) for side in range(2)]

    @pl.when(step == 0)
    def _():
        wide_ref[...] = mix_ref[...].astype(jnp.float32)
        for d in range(outer_width):
            mixed_ref[:, d * pair_width : (d + 1) * pair_width] = wide_ref[
                pl.ds(d, outer_width, stride=outer_width), :
            ].astype(jnp.bfloat16)
        for n in range(4):
            part = proj_ref[:, n * pair_width : (n + 1) * pair_width].astype(jnp.float32)
            weight_ref[n * pair_width : (n + 1) * pair_width, :] = part.T.astype(jnp.bfloat16)
        weight_ref[4 * pair_width :, :] = logit_ref[...].astype(jnp.float32).T.astype(jnp.bfloat16)

    spread = jnp.dot(row_ref[...], mixed_ref[...], preferred_element_type=jnp.float32).astype(
        jnp.bfloat16
    )
    updates = []
    for first in range(0, step_rows, 2):
        both = []
        for k in range(first, min(first + 2, step_rows)):
            piece = spread[k * samples : (k + 1) * samples]
            both.append(
                jnp.concatenate(
                    [piece[:, d * pair_width : (d + 1) * pair_width] for d in order], axis=0
                )
            )
        update = jnp.dot(
            column_ref[...], jnp.concatenate(both, axis=1), preferred_element_type=jnp.float32
        )
        for k in range(len(both)):
            updates.append(update[:, k * pair_width : (k + 1) * pair_width])
    for k in range(step_rows):
        update = updates[k]
        pair_one = (grid_ref[k].astype(jnp.float32) + update * (1.0 / samples)).astype(jnp.bfloat16)
        one_ref[k] = pair_one
        pair_norm = normalize(pair_one, 1).astype(jnp.bfloat16)
        norm_ref[k] = pair_norm
        projected = lax.dot_general(
            weight_ref[...],
            pair_norm,
            (((1,), (1,)), ((), ())),
            preferred_element_type=jnp.float32,
        )
        mask = mask_ref[k]
        row = step * step_rows + k
        for side in range(2):
            base = 2 * side * pair_width
            gate = projected[base : base + pair_width]
            value = projected[base + pair_width : base + 2 * pair_width]
            held_ref[side, pl.ds(row, pair_width, stride=tok_row), :] = (
                jax.nn.sigmoid(gate) * value * mask
            )
        score_ref[k] = jnp.exp(projected[4 * pair_width : 4 * pair_width + head_count])

    @pl.when(step == steps - 1)
    def _():
        devices, _, group, _, tok_col = factor_ref.shape
        for side in range(2):
            factor_ref[:, side] = (
                held_ref[side].astype(jnp.bfloat16).reshape(devices, group, tok_row, tok_col)
            )


def pair_stage(columns, rows, outer_mix, pair_grid, triangle_proj, pair_logit, pair_mask, devices):
    tok_row, tok_col, pair_width = pair_grid.shape
    outer_width = rows.shape[1]
    samples = rows.shape[0] // tok_row
    head_count = pair_logit.shape[1]
    step_rows = 4 if tok_row % 4 == 0 else 1
    steps = tok_row // step_rows
    group = pair_width // devices
    whole = lambda *shape: pl.BlockSpec(shape, lambda r: (0,) * len(shape))
    part = lambda *shape: pl.BlockSpec(shape, lambda r: (r,) + (0,) * (len(shape) - 1))
    return pl.pallas_call(
        functools.partial(pair_kernel, steps, step_rows, samples, head_count),
        grid=(steps,),
        out_shape=(
            jax.ShapeDtypeStruct(pair_grid.shape, jnp.bfloat16),
            jax.ShapeDtypeStruct(pair_grid.shape, jnp.bfloat16),
            jax.ShapeDtypeStruct((tok_row, head_count, tok_col), jnp.float32),
            jax.ShapeDtypeStruct((devices, 2, group, tok_row, tok_col), jnp.bfloat16),
        ),
        in_specs=[
            whole(*columns.shape),
            part(step_rows * samples, outer_width),
            whole(*outer_mix.shape),
            part(step_rows, tok_col, pair_width),
            whole(*triangle_proj.shape),
            whole(*pair_logit.shape),
            part(step_rows, 1, tok_col),
        ],
        out_specs=(
            part(step_rows, tok_col, pair_width),
            part(step_rows, tok_col, pair_width),
            part(step_rows, head_count, tok_col),
            whole(devices, 2, group, tok_row, tok_col),
        ),
        scratch_shapes=[
            pltpu.VMEM((2, pair_width * tok_row, tok_col), jnp.float32),
            pltpu.VMEM(outer_mix.shape, jnp.float32),
            pltpu.VMEM((outer_width, outer_width * pair_width), jnp.bfloat16),
            pltpu.VMEM((4 * pair_width + head_count, pair_width), jnp.bfloat16),
        ],
        name="pair_stage",
    )(columns, rows, outer_mix, pair_grid, triangle_proj, pair_logit, pair_mask[:, None, :])


def tail_kernel(
    step_rows, product_ref, one_ref, gate_ref, mix_ref, up_ref, down_ref, out_ref, held_ref
):
    step = pl.program_id(0)
    devices, group, tok_row, tok_col = product_ref.shape
    pair_width = devices * group
    inner_width = down_ref.shape[0]

    @pl.when(step == 0)
    def _():
        held_ref[...] = (
            product_ref[...].astype(jnp.float32).reshape(pair_width * tok_row, tok_col)
        )

    rows = []
    for k in range(step_rows):
        product = held_ref[pl.ds(step * step_rows + k, pair_width, stride=tok_row), :]
        normed = normalize(product, 0).astype(jnp.bfloat16)
        mixed = lax.dot_general(
            normed, mix_ref[...], (((0,), (0,)), ((), ())), preferred_element_type=jnp.float32
        )
        rows.append((one_ref[k].astype(jnp.float32) + gate_ref[k] * mixed).astype(jnp.bfloat16))
    pair_two = jnp.concatenate(rows, axis=0)
    normed = normalize(pair_two, 1).astype(jnp.bfloat16)
    expanded = jnp.dot(normed, up_ref[...], preferred_element_type=jnp.float32)
    hidden = (jax.nn.silu(expanded[:, :inner_width]) * expanded[:, inner_width:]).astype(
        jnp.bfloat16
    )
    result = (
        pair_two.astype(jnp.float32)
        + jnp.dot(hidden, down_ref[...], preferred_element_type=jnp.float32)
    ).astype(jnp.bfloat16)
    for k in range(step_rows):
        out_ref[k] = result[k * tok_col : (k + 1) * tok_col]


def tail_stage(product, pair_one, gate_out, triangle_mix, transition_up, transition_down):
    tok_row, tok_col, pair_width = pair_one.shape
    step_rows = 4 if tok_row % 4 == 0 else 1
    whole = lambda *shape: pl.BlockSpec(shape, lambda r: (0,) * len(shape))
    part = lambda *shape: pl.BlockSpec(shape, lambda r: (r,) + (0,) * (len(shape) - 1))
    block = part(step_rows, tok_col, pair_width)
    return pl.pallas_call(
        functools.partial(tail_kernel, step_rows),
        grid=(tok_row // step_rows,),
        out_shape=jax.ShapeDtypeStruct(pair_one.shape, jnp.bfloat16),
        in_specs=[
            whole(*product.shape),
            block,
            block,
            whole(*triangle_mix.shape),
            whole(*transition_up.shape),
            whole(*transition_down.shape),
        ],
        out_specs=block,
        scratch_shapes=[pltpu.VMEM((pair_width * tok_row, tok_col), jnp.float32)],
        name="tail_stage",
    )(product, pair_one, gate_out, triangle_mix, transition_up, transition_down)


def on_device(
    pair_grid,
    alignment_pool,
    sample_index,
    token_mask,
    outer_proj,
    outer_mix,
    pair_logit,
    average_proj,
    average_mix,
    triangle_proj,
    triangle_mix,
    transition_up,
    transition_down,
):
    n_row = lax.axis_size("row")
    n_col = lax.axis_size("col")
    tok_row = pair_grid.shape[0]
    tok_col = pair_grid.shape[1]
    pair_width = pair_grid.shape[2]
    samples = sample_index.shape[0]
    align_width = alignment_pool.shape[2]
    head_count = pair_logit.shape[1]
    head_total = average_proj.shape[1] // 2
    head_dim = head_total // head_count
    row_start = lax.axis_index("row") * tok_row
    column_start = lax.axis_index("col") * tok_col
    row_mask = lax.dynamic_slice_in_dim(token_mask, row_start, tok_row, 0).astype(jnp.float32)
    column_mask = lax.dynamic_slice_in_dim(token_mask, column_start, tok_col, 0).astype(jnp.float32)
    pair_mask = row_mask[:, None] * column_mask[None, :]
    alignments, align_norm, rows, column_block = prepare(alignment_pool, sample_index, outer_proj)
    align_rows = align_norm.transpose(1, 0, 2).reshape(samples, tok_row * align_width)
    columns, gathered = gather_blocks(column_block, align_rows)
    columns = columns.reshape(tok_col, column_block.shape[1])
    pair_one, pair_norm, weights, factors = pair_stage(
        columns,
        rows,
        outer_mix,
        pair_grid,
        triangle_proj,
        pair_logit,
        pair_mask,
        n_row * n_col,
    )
    received = lax.all_to_all(factors, ("row", "col"), split_axis=0, concat_axis=0, tiled=True)
    column_norm = (
        gathered.reshape(n_row // n_col, samples, tok_row, align_width)
        .transpose(1, 0, 2, 3)
        .reshape(samples, tok_col, align_width)
    )
    value_weight = average_proj[:, :head_total].reshape(align_width, head_count, head_dim)
    gate_weight = average_proj[:, head_total:].reshape(align_width, head_count, head_dim)
    mix_weight = average_mix.reshape(head_count, head_dim, align_width)
    weights = weights.transpose(1, 0, 2)
    partial_total = jnp.sum(weights, axis=2)
    weights_low = weights.astype(jnp.bfloat16)
    column_values = jnp.einsum(
        "sjm,mhc->hjsc", column_norm, value_weight, preferred_element_type=jnp.float32
    )
    column_values = column_values.astype(jnp.bfloat16).reshape(
        head_count, tok_col, samples * head_dim
    )
    partial_sum = jnp.einsum(
        "hij,hjk->hik", weights_low, column_values, preferred_element_type=jnp.float32
    )
    weighted = sum_columns(partial_sum, jnp.bfloat16)
    totals = sum_columns(partial_total, jnp.float32)
    gate_values = jax.nn.sigmoid(
        jnp.einsum("ism,mhc->hisc", align_norm, gate_weight, preferred_element_type=jnp.float32)
    )
    weighted = weighted.reshape(head_count, tok_row, samples, head_dim)
    averaged = (gate_values * weighted / totals[:, :, None, None]).astype(jnp.bfloat16)
    align_update = jnp.einsum(
        "hisc,hcm->sim", averaged, mix_weight, preferred_element_type=jnp.float32
    )
    alignment_next = (
        alignments.transpose(1, 0, 2).astype(jnp.float32) + align_update
    ).astype(jnp.bfloat16)
    flat_result = triangle_product(received, n_row, n_col)
    product = lax.all_to_all(flat_result, ("row", "col"), split_axis=0, concat_axis=0, tiled=True)
    gate_out = jax.nn.sigmoid(
        jnp.dot(pair_norm, triangle_proj[:, 4 * pair_width :], preferred_element_type=jnp.float32)
    )
    pair_next = tail_stage(
        product, pair_one, gate_out, triangle_mix, transition_up, transition_down
    )
    return (pair_next, alignment_next)


def solution(mesh):
    in_specs = (
        P(("groups", "row"), "col", None),
        P("groups", "row", None),
        P("groups"),
        P("groups"),
        P(),
        P(),
        P(),
        P(),
        P(),
        P(),
        P(),
        P(),
        P(),
    )
    out_specs = (P(("groups", "row"), "col", None), P("groups", "row", None))
    return jax.shard_map(
        on_device, mesh=mesh, in_specs=in_specs, out_specs=out_specs, check_vma=False
    )
```

```python
import functools

import jax
import jax.numpy as jnp
from jax import lax
from jax.experimental import pallas as pl
from jax.experimental.pallas import tpu as pltpu
from jax.sharding import PartitionSpec as P

epsilon = 1e-05


def normalize(values, channel_dim):
    values = values.astype(jnp.float32)
    centred = values - jnp.mean(values, axis=channel_dim, keepdims=True)
    spread = jnp.mean(centred * centred, axis=channel_dim, keepdims=True)
    return centred * lax.rsqrt(spread + epsilon)


def gather_kernel(n_row, n_col, count, *refs):
    blocks, outs = refs[:count], refs[count : 2 * count]
    own_sem, send_sems, far_sems, recv_sems = refs[2 * count :]
    span = n_row // n_col
    row = lax.axis_index("row")
    col = lax.axis_index("col")
    band = row // span
    place = lax.rem(row, span)
    parity = lax.rem(place, 2)
    base = band * span
    twin_place = place + 1 - 2 * parity
    is_source = band == col
    half = span // 2

    def other_band(k):
        return lax.rem(band + k, n_col) * span + place

    def peer_place(k):
        return lax.rem(place + 2 * k, span)

    barrier = pltpu.get_barrier_semaphore()
    for k in range(1, n_col):
        pl.semaphore_signal(barrier, inc=1, device_id={"row": other_band(k)})
    pl.semaphore_signal(barrier, inc=1, device_id={"row": base + twin_place})
    for k in range(1, half):
        pl.semaphore_signal(barrier, inc=1, device_id={"row": base + peer_place(k)})
    pl.semaphore_wait(barrier, n_col - 1 + half)

    def push(n, source, slot, sem, target):
        return pltpu.make_async_remote_copy(
            src_ref=source,
            dst_ref=outs[n].at[slot],
            send_sem=sem,
            recv_sem=recv_sems.at[n, slot],
            device_id={"row": target},
        )

    def far(n, k):
        return push(n, blocks[n], place, far_sems.at[n, k - 1], other_band(k))

    def own_copy(n):
        return pltpu.make_async_copy(blocks[n], outs[n].at[place], own_sem.at[n])

    def arrival(n, slot):
        return push(n, outs[n].at[place], slot, own_sem.at[n], base + twin_place)

    @pl.when(is_source)
    def _():
        for n in range(count):
            for k in range(1, n_col):
                far(n, k).start()
            own_copy(n).start()
        for n in range(count):
            own_copy(n).wait()

    sent = []
    for n in range(count):

        @pl.when(jnp.logical_not(is_source))
        def _():
            arrival(n, place).wait_recv()

        mine = outs[n].at[place]
        near = [
            push(n, mine, place, send_sems.at[n, k - 1], base + peer_place(k))
            for k in range(1, half)
        ]
        near.append(push(n, mine, place, send_sems.at[n, half - 1], base + twin_place))
        for copy in near:
            copy.start()
        sent += near
    for n in range(count):
        for k in range(1, half):
            came = lax.rem(place - 2 * k + span, span)
            arrival(n, came).wait_recv()
            onward = push(
                n, outs[n].at[came], came, send_sems.at[n, half - 1 + k], base + twin_place
            )
            onward.start()
            sent.append(onward)
    for n in range(count):
        for k in range(half):
            arrival(n, lax.rem(twin_place + 2 * k, span)).wait_recv()
    for copy in sent:
        copy.wait_send()

    @pl.when(is_source)
    def _():
        for n in range(count):
            for k in range(1, n_col):
                far(n, k).wait_send()


def gather_blocks(*blocks):
    n_row = lax.axis_size("row")
    n_col = lax.axis_size("col")
    span = n_row // n_col
    count = len(blocks)
    return pl.pallas_call(
        functools.partial(gather_kernel, n_row, n_col, count),
        out_shape=tuple(
            jax.ShapeDtypeStruct((span,) + block.shape, block.dtype) for block in blocks
        ),
        in_specs=[pl.BlockSpec(memory_space=pltpu.VMEM)] * count,
        out_specs=tuple(pl.BlockSpec(memory_space=pltpu.VMEM) for _ in blocks),
        scratch_shapes=[
            pltpu.SemaphoreType.DMA((count,)),
            pltpu.SemaphoreType.DMA((count, span)),
            pltpu.SemaphoreType.DMA((count, max(n_col - 1, 1))),
            pltpu.SemaphoreType.DMA((count, span)),
        ],
        compiler_params=pltpu.CompilerParams(collective_id=0, has_side_effects=True),
        name="gather_blocks",
    )(*blocks)


def sum_columns(values, wire_dtype):
    n_col = lax.axis_size("col")
    total = values
    sent = values.astype(wire_dtype)
    for shift in range(1, n_col):
        pairs = [(k, (k + shift) % n_col) for k in range(n_col)]
        total = total + lax.ppermute(sent, "col", pairs).astype(jnp.float32)
    return total


def exchange_kernel(
    n_row,
    n_col,
    sent_ref,
    out_ref,
    received_ref,
    left_ref,
    right_ref,
    own_sem,
    send_sems,
    recv_sems,
):
    devices = n_row * n_col
    me = lax.axis_index("row") * n_col + lax.axis_index("col")
    barrier = pltpu.get_barrier_semaphore()

    def place(k):
        target = lax.rem(me + k, devices)
        return {"row": target // n_col, "col": lax.rem(target, n_col)}

    def greet(k, carry):
        pl.semaphore_signal(barrier, inc=1, device_id=place(k))
        return carry

    def outgoing(k):
        return pltpu.make_async_remote_copy(
            src_ref=sent_ref.at[lax.rem(me + k, devices)],
            dst_ref=received_ref.at[me],
            send_sem=send_sems.at[k],
            recv_sem=recv_sems.at[k],
            device_id=place(k),
        )

    def incoming(k):
        return pltpu.make_async_remote_copy(
            src_ref=sent_ref.at[me],
            dst_ref=received_ref.at[lax.rem(me - k + devices, devices)],
            send_sem=send_sems.at[k],
            recv_sem=recv_sems.at[k],
            device_id=place(k),
        )

    def start(k, carry):
        outgoing(k).start()
        return carry

    def finish(k, carry):
        outgoing(k).wait_send()
        incoming(k).wait_recv()
        return carry

    own = pltpu.make_async_copy(sent_ref.at[me], received_ref.at[me], own_sem)
    lax.fori_loop(1, devices, greet, 0)
    own.start()
    pl.semaphore_wait(barrier, devices - 1)
    lax.fori_loop(1, devices, start, 0)
    own.wait()
    lax.fori_loop(1, devices, finish, 0)
    _, _, items, tok_row, tok_col = received_ref.shape
    for item in range(items):
        for r in range(n_row):
            for u in range(n_col):
                rows = slice(r * tok_row, (r + 1) * tok_row)
                lanes = slice(u * tok_col, (u + 1) * tok_col)
                left_ref[rows, lanes] = received_ref[r * n_col + u, 0, item]
                right_ref[rows, lanes] = received_ref[r * n_col + u, 1, item]
        result = lax.dot_general(
            left_ref[...],
            right_ref[...],
            (((1,), (1,)), ((), ())),
            preferred_element_type=jnp.float32,
        ).astype(jnp.bfloat16)
        for r in range(n_row):
            for u in range(n_col):
                rows = slice(r * tok_row, (r + 1) * tok_row)
                lanes = slice(u * tok_col, (u + 1) * tok_col)
                out_ref[r * n_col + u, item] = result[rows, lanes]


def exchange_product(factors):
    n_row = lax.axis_size("row")
    n_col = lax.axis_size("col")
    devices, _, items, tok_row, tok_col = factors.shape
    square = (n_row * tok_row, n_col * tok_col)
    return pl.pallas_call(
        functools.partial(exchange_kernel, n_row, n_col),
        out_shape=jax.ShapeDtypeStruct((devices, items, tok_row, tok_col), jnp.bfloat16),
        in_specs=[pl.BlockSpec(memory_space=pltpu.VMEM)],
        out_specs=pl.BlockSpec(memory_space=pltpu.VMEM),
        scratch_shapes=[
            pltpu.VMEM(factors.shape, jnp.bfloat16),
            pltpu.VMEM(square, jnp.bfloat16),
            pltpu.VMEM(square, jnp.bfloat16),
            pltpu.SemaphoreType.DMA,
            pltpu.SemaphoreType.DMA((devices,)),
            pltpu.SemaphoreType.DMA((devices,)),
        ],
        compiler_params=pltpu.CompilerParams(collective_id=1, has_side_effects=True),
        name="exchange_product",
    )(factors)


def prep_kernel(
    index_ref, pool_ref, proj_ref, align_ref, norm_ref, row_ref, column_ref, held_ref
):
    tok_row, align_width, stored = pool_ref.shape
    samples = align_ref.shape[1]
    outer_width = proj_ref.shape[1] // 2
    half = outer_width // 2
    slots = lax.broadcasted_iota(jnp.int32, (stored, samples), 0)
    picks = (slots == index_ref[...]).astype(jnp.float32).T.astype(jnp.bfloat16)
    lanes = lax.broadcasted_iota(jnp.int32, (half, 2 * samples), 1)
    row_weight = proj_ref[:, :outer_width]
    column_weight = proj_ref[...].astype(jnp.float32).T[outer_width:].astype(jnp.bfloat16)
    for t in range(tok_row):
        chosen = lax.dot_general(
            picks, pool_ref[t], (((1,), (1,)), ((), ())), preferred_element_type=jnp.float32
        )
        normed = normalize(chosen, 1).astype(jnp.bfloat16)
        align_ref[t] = chosen.astype(jnp.bfloat16)
        norm_ref[t] = normed
        row_ref[t * samples : (t + 1) * samples, :] = jnp.dot(
            normed, row_weight, preferred_element_type=jnp.float32
        ).astype(jnp.bfloat16)
        factor = lax.dot_general(
            column_weight,
            jnp.concatenate([normed, normed], axis=0),
            (((1,), (1,)), ((), ())),
            preferred_element_type=jnp.float32,
        )
        held_ref[t * half : (t + 1) * half, :] = jnp.where(
            lanes < samples, factor[:half], factor[half:]
        )
    for d in range(half):
        column_ref[:, d * 2 * samples : (d + 1) * 2 * samples] = held_ref[
            pl.ds(d, tok_row, stride=half), :
        ].astype(jnp.bfloat16)


def prepare(alignment_pool, sample_index, outer_proj):
    stored, tok_row, align_width = alignment_pool.shape
    samples = sample_index.shape[0]
    outer_width = outer_proj.shape[1] // 2
    half = outer_width // 2
    return pl.pallas_call(
        prep_kernel,
        out_shape=(
            jax.ShapeDtypeStruct((tok_row, samples, align_width), jnp.bfloat16),
            jax.ShapeDtypeStruct((tok_row, samples, align_width), jnp.bfloat16),
            jax.ShapeDtypeStruct((tok_row * samples, outer_width), jnp.bfloat16),
            jax.ShapeDtypeStruct((tok_row, outer_width * samples), jnp.bfloat16),
        ),
        scratch_shapes=[pltpu.VMEM((tok_row * half, 2 * samples), jnp.float32)],
        name="prepare",
    )(sample_index[None, :], alignment_pool.transpose(1, 2, 0), outer_proj)


def pair_kernel(
    steps,
    step_rows,
    samples,
    head_count,
    column_ref,
    row_ref,
    mix_ref,
    grid_ref,
    proj_ref,
    logit_ref,
    mask_ref,
    one_ref,
    norm_ref,
    score_ref,
    factor_ref,
    held_ref,
    wide_ref,
    mixed_ref,
    weight_ref,
):
    step = pl.program_id(0)
    pair_width = grid_ref.shape[2]
    outer_width = row_ref.shape[1]
    half = outer_width // 2
    tok_row = steps * step_rows
    order = [side * half + d for d in range(half) for side in range(2)]

    @pl.when(step == 0)
    def _():
        wide_ref[...] = mix_ref[...].astype(jnp.float32)
        for d in range(outer_width):
            mixed_ref[:, d * pair_width : (d + 1) * pair_width] = wide_ref[
                pl.ds(d, outer_width, stride=outer_width), :
            ].astype(jnp.bfloat16)
        for n in range(4):
            part = proj_ref[:, n * pair_width : (n + 1) * pair_width].astype(jnp.float32)
            weight_ref[n * pair_width : (n + 1) * pair_width, :] = part.T.astype(jnp.bfloat16)
        weight_ref[4 * pair_width :, :] = logit_ref[...].astype(jnp.float32).T.astype(jnp.bfloat16)

    spread = jnp.dot(row_ref[...], mixed_ref[...], preferred_element_type=jnp.float32).astype(
        jnp.bfloat16
    )
    updates = []
    for first in range(0, step_rows, 2):
        both = []
        for k in range(first, min(first + 2, step_rows)):
            piece = spread[k * samples : (k + 1) * samples]
            both.append(
                jnp.concatenate(
                    [piece[:, d * pair_width : (d + 1) * pair_width] for d in order], axis=0
                )
            )
        update = jnp.dot(
            column_ref[...], jnp.concatenate(both, axis=1), preferred_element_type=jnp.float32
        )
        for k in range(len(both)):
            updates.append(update[:, k * pair_width : (k + 1) * pair_width])
    for k in range(step_rows):
        update = updates[k]
        pair_one = (grid_ref[k].astype(jnp.float32) + update * (1.0 / samples)).astype(jnp.bfloat16)
        one_ref[k] = pair_one
        pair_norm = normalize(pair_one, 1).astype(jnp.bfloat16)
        norm_ref[k] = pair_norm
        projected = lax.dot_general(
            weight_ref[...],
            pair_norm,
            (((1,), (1,)), ((), ())),
            preferred_element_type=jnp.float32,
        )
        mask = mask_ref[k]
        row = step * step_rows + k
        for side in range(2):
            base = 2 * side * pair_width
            gate = projected[base : base + pair_width]
            value = projected[base + pair_width : base + 2 * pair_width]
            held_ref[side, pl.ds(row, pair_width, stride=tok_row), :] = (
                jax.nn.sigmoid(gate) * value * mask
            )
        score_ref[k] = jnp.exp(projected[4 * pair_width : 4 * pair_width + head_count])

    @pl.when(step == steps - 1)
    def _():
        devices, _, group, _, tok_col = factor_ref.shape
        for side in range(2):
            factor_ref[:, side] = (
                held_ref[side].astype(jnp.bfloat16).reshape(devices, group, tok_row, tok_col)
            )


def pair_stage(columns, rows, outer_mix, pair_grid, triangle_proj, pair_logit, pair_mask, devices):
    tok_row, tok_col, pair_width = pair_grid.shape
    outer_width = rows.shape[1]
    samples = rows.shape[0] // tok_row
    head_count = pair_logit.shape[1]
    step_rows = 4 if tok_row % 4 == 0 else 1
    steps = tok_row // step_rows
    group = pair_width // devices
    whole = lambda *shape: pl.BlockSpec(shape, lambda r: (0,) * len(shape))
    part = lambda *shape: pl.BlockSpec(shape, lambda r: (r,) + (0,) * (len(shape) - 1))
    return pl.pallas_call(
        functools.partial(pair_kernel, steps, step_rows, samples, head_count),
        grid=(steps,),
        out_shape=(
            jax.ShapeDtypeStruct(pair_grid.shape, jnp.bfloat16),
            jax.ShapeDtypeStruct(pair_grid.shape, jnp.bfloat16),
            jax.ShapeDtypeStruct((tok_row, head_count, tok_col), jnp.float32),
            jax.ShapeDtypeStruct((devices, 2, group, tok_row, tok_col), jnp.bfloat16),
        ),
        in_specs=[
            whole(*columns.shape),
            part(step_rows * samples, outer_width),
            whole(*outer_mix.shape),
            part(step_rows, tok_col, pair_width),
            whole(*triangle_proj.shape),
            whole(*pair_logit.shape),
            part(step_rows, 1, tok_col),
        ],
        out_specs=(
            part(step_rows, tok_col, pair_width),
            part(step_rows, tok_col, pair_width),
            part(step_rows, head_count, tok_col),
            whole(devices, 2, group, tok_row, tok_col),
        ),
        scratch_shapes=[
            pltpu.VMEM((2, pair_width * tok_row, tok_col), jnp.float32),
            pltpu.VMEM(outer_mix.shape, jnp.float32),
            pltpu.VMEM((outer_width, outer_width * pair_width), jnp.bfloat16),
            pltpu.VMEM((4 * pair_width + head_count, pair_width), jnp.bfloat16),
        ],
        name="pair_stage",
    )(columns, rows, outer_mix, pair_grid, triangle_proj, pair_logit, pair_mask[:, None, :])


def tail_kernel(
    step_rows, product_ref, one_ref, gate_ref, mix_ref, up_ref, down_ref, out_ref, held_ref
):
    step = pl.program_id(0)
    devices, group, tok_row, tok_col = product_ref.shape
    pair_width = devices * group
    inner_width = down_ref.shape[0]

    @pl.when(step == 0)
    def _():
        held_ref[...] = (
            product_ref[...].astype(jnp.float32).reshape(pair_width * tok_row, tok_col)
        )

    rows = []
    for k in range(step_rows):
        product = held_ref[pl.ds(step * step_rows + k, pair_width, stride=tok_row), :]
        normed = normalize(product, 0).astype(jnp.bfloat16)
        mixed = lax.dot_general(
            normed, mix_ref[...], (((0,), (0,)), ((), ())), preferred_element_type=jnp.float32
        )
        rows.append((one_ref[k].astype(jnp.float32) + gate_ref[k] * mixed).astype(jnp.bfloat16))
    pair_two = jnp.concatenate(rows, axis=0)
    normed = normalize(pair_two, 1).astype(jnp.bfloat16)
    expanded = jnp.dot(normed, up_ref[...], preferred_element_type=jnp.float32)
    hidden = (jax.nn.silu(expanded[:, :inner_width]) * expanded[:, inner_width:]).astype(
        jnp.bfloat16
    )
    result = (
        pair_two.astype(jnp.float32)
        + jnp.dot(hidden, down_ref[...], preferred_element_type=jnp.float32)
    ).astype(jnp.bfloat16)
    for k in range(step_rows):
        out_ref[k] = result[k * tok_col : (k + 1) * tok_col]


def tail_stage(product, pair_one, gate_out, triangle_mix, transition_up, transition_down):
    tok_row, tok_col, pair_width = pair_one.shape
    step_rows = 4 if tok_row % 4 == 0 else 1
    whole = lambda *shape: pl.BlockSpec(shape, lambda r: (0,) * len(shape))
    part = lambda *shape: pl.BlockSpec(shape, lambda r: (r,) + (0,) * (len(shape) - 1))
    block = part(step_rows, tok_col, pair_width)
    return pl.pallas_call(
        functools.partial(tail_kernel, step_rows),
        grid=(tok_row // step_rows,),
        out_shape=jax.ShapeDtypeStruct(pair_one.shape, jnp.bfloat16),
        in_specs=[
            whole(*product.shape),
            block,
            block,
            whole(*triangle_mix.shape),
            whole(*transition_up.shape),
            whole(*transition_down.shape),
        ],
        out_specs=block,
        scratch_shapes=[pltpu.VMEM((pair_width * tok_row, tok_col), jnp.float32)],
        name="tail_stage",
    )(product, pair_one, gate_out, triangle_mix, transition_up, transition_down)


def on_device(
    pair_grid,
    alignment_pool,
    sample_index,
    token_mask,
    outer_proj,
    outer_mix,
    pair_logit,
    average_proj,
    average_mix,
    triangle_proj,
    triangle_mix,
    transition_up,
    transition_down,
):
    n_row = lax.axis_size("row")
    n_col = lax.axis_size("col")
    tok_row = pair_grid.shape[0]
    tok_col = pair_grid.shape[1]
    pair_width = pair_grid.shape[2]
    samples = sample_index.shape[0]
    align_width = alignment_pool.shape[2]
    head_count = pair_logit.shape[1]
    head_total = average_proj.shape[1] // 2
    head_dim = head_total // head_count
    row_start = lax.axis_index("row") * tok_row
    column_start = lax.axis_index("col") * tok_col
    row_mask = lax.dynamic_slice_in_dim(token_mask, row_start, tok_row, 0).astype(jnp.float32)
    column_mask = lax.dynamic_slice_in_dim(token_mask, column_start, tok_col, 0).astype(jnp.float32)
    pair_mask = row_mask[:, None] * column_mask[None, :]
    alignments, align_norm, rows, column_block = prepare(alignment_pool, sample_index, outer_proj)
    align_rows = align_norm.transpose(1, 0, 2).reshape(samples, tok_row * align_width)
    columns, gathered = gather_blocks(column_block, align_rows)
    columns = columns.reshape(tok_col, column_block.shape[1])
    pair_one, pair_norm, weights, factors = pair_stage(
        columns,
        rows,
        outer_mix,
        pair_grid,
        triangle_proj,
        pair_logit,
        pair_mask,
        n_row * n_col,
    )
    flat_result = exchange_product(factors)
    flat_result, weights, gathered = lax.optimization_barrier((flat_result, weights, gathered))
    column_norm = (
        gathered.reshape(n_row // n_col, samples, tok_row, align_width)
        .transpose(1, 0, 2, 3)
        .reshape(samples, tok_col, align_width)
    )
    value_weight = average_proj[:, :head_total].reshape(align_width, head_count, head_dim)
    gate_weight = average_proj[:, head_total:].reshape(align_width, head_count, head_dim)
    mix_weight = average_mix.reshape(head_count, head_dim, align_width)
    weights = weights.transpose(1, 0, 2)
    partial_total = jnp.sum(weights, axis=2)
    weights_low = weights.astype(jnp.bfloat16)
    column_values = jnp.einsum(
        "sjm,mhc->hjsc", column_norm, value_weight, preferred_element_type=jnp.float32
    )
    column_values = column_values.astype(jnp.bfloat16).reshape(
        head_count, tok_col, samples * head_dim
    )
    partial_sum = jnp.einsum(
        "hij,hjk->hik", weights_low, column_values, preferred_element_type=jnp.float32
    )
    weighted = sum_columns(partial_sum, jnp.bfloat16)
    totals = sum_columns(partial_total, jnp.float32)
    gate_values = jax.nn.sigmoid(
        jnp.einsum("ism,mhc->hisc", align_norm, gate_weight, preferred_element_type=jnp.float32)
    )
    weighted = weighted.reshape(head_count, tok_row, samples, head_dim)
    averaged = (gate_values * weighted / totals[:, :, None, None]).astype(jnp.bfloat16)
    align_update = jnp.einsum(
        "hisc,hcm->sim", averaged, mix_weight, preferred_element_type=jnp.float32
    )
    alignment_next = (
        alignments.transpose(1, 0, 2).astype(jnp.float32) + align_update
    ).astype(jnp.bfloat16)
    product = lax.all_to_all(flat_result, ("row", "col"), split_axis=0, concat_axis=0, tiled=True)
    gate_out = jax.nn.sigmoid(
        jnp.dot(pair_norm, triangle_proj[:, 4 * pair_width :], preferred_element_type=jnp.float32)
    )
    pair_next = tail_stage(
        product, pair_one, gate_out, triangle_mix, transition_up, transition_down
    )
    return (pair_next, alignment_next)


def solution(mesh):
    in_specs = (
        P(("groups", "row"), "col", None),
        P("groups", "row", None),
        P("groups"),
        P("groups"),
        P(),
        P(),
        P(),
        P(),
        P(),
        P(),
        P(),
        P(),
        P(),
    )
    out_specs = (P(("groups", "row"), "col", None), P("groups", "row", None))
    return jax.shard_map(
        on_device, mesh=mesh, in_specs=in_specs, out_specs=out_specs, check_vma=False
    )
```

```python
import functools

import jax
import jax.numpy as jnp
from jax import lax
from jax.experimental import pallas as pl
from jax.experimental.pallas import tpu as pltpu
from jax.sharding import PartitionSpec as P

epsilon = 1e-05


def normalize(values, channel_dim):
    values = values.astype(jnp.float32)
    centred = values - jnp.mean(values, axis=channel_dim, keepdims=True)
    spread = jnp.mean(centred * centred, axis=channel_dim, keepdims=True)
    return centred * lax.rsqrt(spread + epsilon)


def gather_kernel(n_row, n_col, count, *refs):
    blocks, outs = refs[:count], refs[count : 2 * count]
    own_sem, send_sems, far_sems, recv_sems = refs[2 * count :]
    span = n_row // n_col
    row = lax.axis_index("row")
    col = lax.axis_index("col")
    band = row // span
    place = lax.rem(row, span)
    parity = lax.rem(place, 2)
    base = band * span
    twin_place = place + 1 - 2 * parity
    is_source = band == col
    half = span // 2

    def other_band(k):
        return lax.rem(band + k, n_col) * span + place

    def peer_place(k):
        return lax.rem(place + 2 * k, span)

    barrier = pltpu.get_barrier_semaphore()
    for k in range(1, n_col):
        pl.semaphore_signal(barrier, inc=1, device_id={"row": other_band(k)})
    pl.semaphore_signal(barrier, inc=1, device_id={"row": base + twin_place})
    for k in range(1, half):
        pl.semaphore_signal(barrier, inc=1, device_id={"row": base + peer_place(k)})
    pl.semaphore_wait(barrier, n_col - 1 + half)

    def push(n, source, slot, sem, target):
        return pltpu.make_async_remote_copy(
            src_ref=source,
            dst_ref=outs[n].at[slot],
            send_sem=sem,
            recv_sem=recv_sems.at[n, slot],
            device_id={"row": target},
        )

    def far(n, k):
        return push(n, blocks[n], place, far_sems.at[n, k - 1], other_band(k))

    def own_copy(n):
        return pltpu.make_async_copy(blocks[n], outs[n].at[place], own_sem.at[n])

    def arrival(n, slot):
        return push(n, outs[n].at[place], slot, own_sem.at[n], base + twin_place)

    @pl.when(is_source)
    def _():
        for n in range(count):
            for k in range(1, n_col):
                far(n, k).start()
            own_copy(n).start()
        for n in range(count):
            own_copy(n).wait()

    sent = []
    for n in range(count):

        @pl.when(jnp.logical_not(is_source))
        def _():
            arrival(n, place).wait_recv()

        mine = outs[n].at[place]
        near = [
            push(n, mine, place, send_sems.at[n, k - 1], base + peer_place(k))
            for k in range(1, half)
        ]
        near.append(push(n, mine, place, send_sems.at[n, half - 1], base + twin_place))
        for copy in near:
            copy.start()
        sent += near
    for n in range(count):
        for k in range(1, half):
            came = lax.rem(place - 2 * k + span, span)
            arrival(n, came).wait_recv()
            onward = push(
                n, outs[n].at[came], came, send_sems.at[n, half - 1 + k], base + twin_place
            )
            onward.start()
            sent.append(onward)
    for n in range(count):
        for k in range(half):
            arrival(n, lax.rem(twin_place + 2 * k, span)).wait_recv()
    for copy in sent:
        copy.wait_send()

    @pl.when(is_source)
    def _():
        for n in range(count):
            for k in range(1, n_col):
                far(n, k).wait_send()


def gather_blocks(*blocks):
    n_row = lax.axis_size("row")
    n_col = lax.axis_size("col")
    span = n_row // n_col
    count = len(blocks)
    return pl.pallas_call(
        functools.partial(gather_kernel, n_row, n_col, count),
        out_shape=tuple(
            jax.ShapeDtypeStruct((span,) + block.shape, block.dtype) for block in blocks
        ),
        in_specs=[pl.BlockSpec(memory_space=pltpu.VMEM)] * count,
        out_specs=tuple(pl.BlockSpec(memory_space=pltpu.VMEM) for _ in blocks),
        scratch_shapes=[
            pltpu.SemaphoreType.DMA((count,)),
            pltpu.SemaphoreType.DMA((count, span)),
            pltpu.SemaphoreType.DMA((count, max(n_col - 1, 1))),
            pltpu.SemaphoreType.DMA((count, span)),
        ],
        compiler_params=pltpu.CompilerParams(collective_id=0, has_side_effects=True),
        name="gather_blocks",
    )(*blocks)


def sum_columns(values, wire_dtype):
    n_col = lax.axis_size("col")
    total = values
    sent = values.astype(wire_dtype)
    for shift in range(1, n_col):
        pairs = [(k, (k + shift) % n_col) for k in range(n_col)]
        total = total + lax.ppermute(sent, "col", pairs).astype(jnp.float32)
    return total


def product_kernel(n_row, n_col, tok_row, tok_col, received_ref, out_ref, left_ref, right_ref):
    for r in range(n_row):
        for u in range(n_col):
            rows = slice(r * tok_row, (r + 1) * tok_row)
            lanes = slice(u * tok_col, (u + 1) * tok_col)
            left_ref[rows, lanes] = received_ref[r * n_col + u, 0, 0]
            right_ref[rows, lanes] = received_ref[r * n_col + u, 1, 0]
    result = lax.dot_general(
        left_ref[...], right_ref[...], (((1,), (1,)), ((), ())), preferred_element_type=jnp.float32
    ).astype(jnp.bfloat16)
    for r in range(n_row):
        for u in range(n_col):
            rows = slice(r * tok_row, (r + 1) * tok_row)
            lanes = slice(u * tok_col, (u + 1) * tok_col)
            out_ref[r * n_col + u, 0] = result[rows, lanes]


def triangle_product(received, n_row, n_col):
    devices, _, items, tok_row, tok_col = received.shape
    length = n_row * tok_row
    return pl.pallas_call(
        functools.partial(product_kernel, n_row, n_col, tok_row, tok_col),
        grid=(items,),
        out_shape=jax.ShapeDtypeStruct((devices, items, tok_row, tok_col), jnp.bfloat16),
        in_specs=[
            pl.BlockSpec((devices, 2, 1, tok_row, tok_col), lambda c: (0, 0, c, 0, 0))
        ],
        out_specs=pl.BlockSpec((devices, 1, tok_row, tok_col), lambda c: (0, c, 0, 0)),
        scratch_shapes=[
            pltpu.VMEM((length, length), jnp.bfloat16),
            pltpu.VMEM((length, length), jnp.bfloat16),
        ],
        name="triangle_product",
    )(received)


def prep_kernel(
    index_ref, pool_ref, proj_ref, align_ref, norm_ref, flat_ref, row_ref, column_ref, held_ref
):
    tok_row, align_width, stored = pool_ref.shape
    samples = align_ref.shape[1]
    outer_width = proj_ref.shape[1] // 2
    half = outer_width // 2
    slots = lax.broadcasted_iota(jnp.int32, (stored, samples), 0)
    picks = (slots == index_ref[...]).astype(jnp.float32).T.astype(jnp.bfloat16)
    lanes = lax.broadcasted_iota(jnp.int32, (half, 2 * samples), 1)
    row_weight = proj_ref[:, :outer_width]
    column_weight = proj_ref[...].astype(jnp.float32).T[outer_width:].astype(jnp.bfloat16)
    for t in range(tok_row):
        chosen = lax.dot_general(
            picks, pool_ref[t], (((1,), (1,)), ((), ())), preferred_element_type=jnp.float32
        )
        normed = normalize(chosen, 1).astype(jnp.bfloat16)
        align_ref[t] = chosen.astype(jnp.bfloat16)
        norm_ref[t] = normed
        flat_ref[:, t * align_width : (t + 1) * align_width] = normed
        row_ref[t * samples : (t + 1) * samples, :] = jnp.dot(
            normed, row_weight, preferred_element_type=jnp.float32
        ).astype(jnp.bfloat16)
        factor = lax.dot_general(
            column_weight,
            jnp.concatenate([normed, normed], axis=0),
            (((1,), (1,)), ((), ())),
            preferred_element_type=jnp.float32,
        )
        held_ref[t * half : (t + 1) * half, :] = jnp.where(
            lanes < samples, factor[:half], factor[half:]
        )
    for d in range(half):
        column_ref[:, d * 2 * samples : (d + 1) * 2 * samples] = held_ref[
            pl.ds(d, tok_row, stride=half), :
        ].astype(jnp.bfloat16)


def prepare(alignment_pool, sample_index, outer_proj):
    stored, tok_row, align_width = alignment_pool.shape
    samples = sample_index.shape[0]
    outer_width = outer_proj.shape[1] // 2
    half = outer_width // 2
    return pl.pallas_call(
        prep_kernel,
        out_shape=(
            jax.ShapeDtypeStruct((tok_row, samples, align_width), jnp.bfloat16),
            jax.ShapeDtypeStruct((tok_row, samples, align_width), jnp.bfloat16),
            jax.ShapeDtypeStruct((samples, tok_row * align_width), jnp.bfloat16),
            jax.ShapeDtypeStruct((tok_row * samples, outer_width), jnp.bfloat16),
            jax.ShapeDtypeStruct((tok_row, outer_width * samples), jnp.bfloat16),
        ),
        scratch_shapes=[pltpu.VMEM((tok_row * half, 2 * samples), jnp.float32)],
        name="prepare",
    )(sample_index[None, :], alignment_pool.transpose(1, 2, 0), outer_proj)


def pair_kernel(
    steps,
    step_rows,
    samples,
    head_count,
    column_ref,
    row_ref,
    mix_ref,
    grid_ref,
    proj_ref,
    logit_ref,
    mark_ref,
    mask_ref,
    one_ref,
    norm_ref,
    score_ref,
    factor_ref,
    held_ref,
    wide_ref,
    mixed_ref,
    weight_ref,
):
    step = pl.program_id(0)
    pair_width = grid_ref.shape[2]
    outer_width = row_ref.shape[1]
    half = outer_width // 2
    tok_row = steps * step_rows
    order = [side * half + d for d in range(half) for side in range(2)]

    @pl.when(step == 0)
    def _():
        wide_ref[...] = mix_ref[...].astype(jnp.float32)
        for d in range(outer_width):
            mixed_ref[:, d * pair_width : (d + 1) * pair_width] = wide_ref[
                pl.ds(d, outer_width, stride=outer_width), :
            ].astype(jnp.bfloat16)
        for n in range(4):
            part = proj_ref[:, n * pair_width : (n + 1) * pair_width].astype(jnp.float32)
            weight_ref[n * pair_width : (n + 1) * pair_width, :] = part.T.astype(jnp.bfloat16)
        weight_ref[4 * pair_width :, :] = logit_ref[...]

    tok_col = grid_ref.shape[1]
    row_start = lax.axis_index("row") * tok_row
    column_start = pl.multiple_of(lax.axis_index("col") * tok_col, tok_col)
    column_mask = mask_ref[:, pl.ds(column_start, tok_col)].astype(jnp.float32)
    spread = jnp.dot(row_ref[...], mixed_ref[...], preferred_element_type=jnp.float32).astype(
        jnp.bfloat16
    )
    updates = []
    for first in range(0, step_rows, 2):
        both = []
        for k in range(first, min(first + 2, step_rows)):
            piece = spread[k * samples : (k + 1) * samples]
            both.append(
                jnp.concatenate(
                    [piece[:, d * pair_width : (d + 1) * pair_width] for d in order], axis=0
                )
            )
        update = jnp.dot(
            column_ref[...], jnp.concatenate(both, axis=1), preferred_element_type=jnp.float32
        )
        for k in range(len(both)):
            updates.append(update[:, k * pair_width : (k + 1) * pair_width])
    for k in range(step_rows):
        update = updates[k]
        pair_one = (grid_ref[k].astype(jnp.float32) + update * (1.0 / samples)).astype(jnp.bfloat16)
        one_ref[k] = pair_one
        pair_norm = normalize(pair_one, 1).astype(jnp.bfloat16)
        norm_ref[k] = pair_norm
        projected = lax.dot_general(
            weight_ref[...],
            pair_norm,
            (((1,), (1,)), ((), ())),
            preferred_element_type=jnp.float32,
        )
        row = step * step_rows + k
        mask = column_mask * mark_ref[row_start + row].astype(jnp.float32)
        for side in range(2):
            base = 2 * side * pair_width
            gate = projected[base : base + pair_width]
            value = projected[base + pair_width : base + 2 * pair_width]
            held_ref[side, pl.ds(row, pair_width, stride=tok_row), :] = (
                jax.nn.sigmoid(gate) * value * mask
            )
        score_ref[k] = jnp.exp(projected[4 * pair_width : 4 * pair_width + head_count])

    @pl.when(step == steps - 1)
    def _():
        devices, _, group, _, tok_col = factor_ref.shape
        for side in range(2):
            factor_ref[:, side] = (
                held_ref[side].astype(jnp.bfloat16).reshape(devices, group, tok_row, tok_col)
            )


def pair_stage(columns, rows, outer_mix, pair_grid, triangle_proj, pair_logit, token_mask, devices):
    tok_row, tok_col, pair_width = pair_grid.shape
    outer_width = rows.shape[1]
    samples = rows.shape[0] // tok_row
    head_count = pair_logit.shape[1]
    step_rows = 4 if tok_row % 4 == 0 else 1
    steps = tok_row // step_rows
    group = pair_width // devices
    whole = lambda *shape: pl.BlockSpec(shape, lambda r: (0,) * len(shape))
    part = lambda *shape: pl.BlockSpec(shape, lambda r: (r,) + (0,) * (len(shape) - 1))
    return pl.pallas_call(
        functools.partial(pair_kernel, steps, step_rows, samples, head_count),
        grid=(steps,),
        out_shape=(
            jax.ShapeDtypeStruct(pair_grid.shape, jnp.bfloat16),
            jax.ShapeDtypeStruct(pair_grid.shape, jnp.bfloat16),
            jax.ShapeDtypeStruct((tok_row, head_count, tok_col), jnp.float32),
            jax.ShapeDtypeStruct((devices, 2, group, tok_row, tok_col), jnp.bfloat16),
        ),
        in_specs=[
            whole(*columns.shape),
            part(step_rows * samples, outer_width),
            whole(*outer_mix.shape),
            part(step_rows, tok_col, pair_width),
            whole(*triangle_proj.shape),
            whole(*pair_logit.shape[::-1]),
            pl.BlockSpec(memory_space=pltpu.SMEM),
            whole(1, token_mask.shape[0]),
        ],
        out_specs=(
            part(step_rows, tok_col, pair_width),
            part(step_rows, tok_col, pair_width),
            part(step_rows, head_count, tok_col),
            whole(devices, 2, group, tok_row, tok_col),
        ),
        scratch_shapes=[
            pltpu.VMEM((2, pair_width * tok_row, tok_col), jnp.float32),
            pltpu.VMEM(outer_mix.shape, jnp.float32),
            pltpu.VMEM((outer_width, outer_width * pair_width), jnp.bfloat16),
            pltpu.VMEM((4 * pair_width + head_count, pair_width), jnp.bfloat16),
        ],
        name="pair_stage",
    )(columns, rows, outer_mix, pair_grid, triangle_proj, pair_logit.T, token_mask, token_mask[None, :])


def tail_kernel(
    step_rows, product_ref, one_ref, gate_ref, mix_ref, up_ref, down_ref, out_ref, held_ref
):
    step = pl.program_id(0)
    devices, group, tok_row, tok_col = product_ref.shape
    pair_width = devices * group
    inner_width = down_ref.shape[0]

    @pl.when(step == 0)
    def _():
        held_ref[...] = (
            product_ref[...].astype(jnp.float32).reshape(pair_width * tok_row, tok_col)
        )

    rows = []
    for k in range(step_rows):
        product = held_ref[pl.ds(step * step_rows + k, pair_width, stride=tok_row), :]
        normed = normalize(product, 0).astype(jnp.bfloat16)
        mixed = lax.dot_general(
            normed, mix_ref[...], (((0,), (0,)), ((), ())), preferred_element_type=jnp.float32
        )
        rows.append((one_ref[k].astype(jnp.float32) + gate_ref[k] * mixed).astype(jnp.bfloat16))
    pair_two = jnp.concatenate(rows, axis=0)
    normed = normalize(pair_two, 1).astype(jnp.bfloat16)
    expanded = jnp.dot(normed, up_ref[...], preferred_element_type=jnp.float32)
    hidden = (jax.nn.silu(expanded[:, :inner_width]) * expanded[:, inner_width:]).astype(
        jnp.bfloat16
    )
    result = (
        pair_two.astype(jnp.float32)
        + jnp.dot(hidden, down_ref[...], preferred_element_type=jnp.float32)
    ).astype(jnp.bfloat16)
    for k in range(step_rows):
        out_ref[k] = result[k * tok_col : (k + 1) * tok_col]


def tail_stage(product, pair_one, gate_out, triangle_mix, transition_up, transition_down):
    tok_row, tok_col, pair_width = pair_one.shape
    step_rows = 4 if tok_row % 4 == 0 else 1
    whole = lambda *shape: pl.BlockSpec(shape, lambda r: (0,) * len(shape))
    part = lambda *shape: pl.BlockSpec(shape, lambda r: (r,) + (0,) * (len(shape) - 1))
    block = part(step_rows, tok_col, pair_width)
    return pl.pallas_call(
        functools.partial(tail_kernel, step_rows),
        grid=(tok_row // step_rows,),
        out_shape=jax.ShapeDtypeStruct(pair_one.shape, jnp.bfloat16),
        in_specs=[
            whole(*product.shape),
            block,
            block,
            whole(*triangle_mix.shape),
            whole(*transition_up.shape),
            whole(*transition_down.shape),
        ],
        out_specs=block,
        scratch_shapes=[pltpu.VMEM((pair_width * tok_row, tok_col), jnp.float32)],
        name="tail_stage",
    )(product, pair_one, gate_out, triangle_mix, transition_up, transition_down)


def on_device(
    pair_grid,
    alignment_pool,
    sample_index,
    token_mask,
    outer_proj,
    outer_mix,
    pair_logit,
    average_proj,
    average_mix,
    triangle_proj,
    triangle_mix,
    transition_up,
    transition_down,
):
    n_row = lax.axis_size("row")
    n_col = lax.axis_size("col")
    tok_row = pair_grid.shape[0]
    tok_col = pair_grid.shape[1]
    pair_width = pair_grid.shape[2]
    samples = sample_index.shape[0]
    align_width = alignment_pool.shape[2]
    head_count = pair_logit.shape[1]
    head_total = average_proj.shape[1] // 2
    head_dim = head_total // head_count
    alignments, align_norm, align_rows, rows, column_block = prepare(
        alignment_pool, sample_index, outer_proj
    )
    columns, gathered = gather_blocks(column_block, align_rows)
    columns = columns.reshape(tok_col, column_block.shape[1])
    pair_one, pair_norm, weights, factors = pair_stage(
        columns,
        rows,
        outer_mix,
        pair_grid,
        triangle_proj,
        pair_logit,
        token_mask,
        n_row * n_col,
    )
    received = lax.all_to_all(factors, ("row", "col"), split_axis=0, concat_axis=0, tiled=True)
    column_norm = (
        gathered.reshape(n_row // n_col, samples, tok_row, align_width)
        .transpose(1, 0, 2, 3)
        .reshape(samples, tok_col, align_width)
    )
    value_weight = average_proj[:, :head_total].reshape(align_width, head_count, head_dim)
    gate_weight = average_proj[:, head_total:].reshape(align_width, head_count, head_dim)
    mix_weight = average_mix.reshape(head_count, head_dim, align_width)
    weights = weights.transpose(1, 0, 2)
    partial_total = jnp.sum(weights, axis=2)
    weights_low = weights.astype(jnp.bfloat16)
    column_values = jnp.einsum(
        "sjm,mhc->hjsc", column_norm, value_weight, preferred_element_type=jnp.float32
    )
    column_values = column_values.astype(jnp.bfloat16).reshape(
        head_count, tok_col, samples * head_dim
    )
    partial_sum = jnp.einsum(
        "hij,hjk->hik", weights_low, column_values, preferred_element_type=jnp.float32
    )
    partial_sum = partial_sum.astype(jnp.bfloat16)
    received, partial_sum, partial_total = lax.optimization_barrier(
        (received, partial_sum, partial_total)
    )
    weighted = sum_columns(partial_sum, jnp.bfloat16)
    totals = sum_columns(partial_total, jnp.float32)
    gate_values = jax.nn.sigmoid(
        jnp.einsum("ism,mhc->hisc", align_norm, gate_weight, preferred_element_type=jnp.float32)
    )
    weighted = weighted.reshape(head_count, tok_row, samples, head_dim)
    averaged = (gate_values * weighted / totals[:, :, None, None]).astype(jnp.bfloat16)
    align_update = jnp.einsum(
        "hisc,hcm->sim", averaged, mix_weight, preferred_element_type=jnp.float32
    )
    alignment_next = (
        alignments.transpose(1, 0, 2).astype(jnp.float32) + align_update
    ).astype(jnp.bfloat16)
    flat_result = triangle_product(received, n_row, n_col)
    product = lax.all_to_all(flat_result, ("row", "col"), split_axis=0, concat_axis=0, tiled=True)
    gate_out = jax.nn.sigmoid(
        jnp.dot(pair_norm, triangle_proj[:, 4 * pair_width :], preferred_element_type=jnp.float32)
    )
    pair_next = tail_stage(
        product, pair_one, gate_out, triangle_mix, transition_up, transition_down
    )
    return (pair_next, alignment_next)


def solution(mesh):
    in_specs = (
        P(("groups", "row"), "col", None),
        P("groups", "row", None),
        P("groups"),
        P("groups"),
        P(),
        P(),
        P(),
        P(),
        P(),
        P(),
        P(),
        P(),
        P(),
    )
    out_specs = (P(("groups", "row"), "col", None), P("groups", "row", None))
    return jax.shard_map(
        on_device, mesh=mesh, in_specs=in_specs, out_specs=out_specs, check_vma=False
    )
```

```python
import functools

import jax
import jax.numpy as jnp
from jax import lax
from jax.experimental import pallas as pl
from jax.experimental.pallas import tpu as pltpu
from jax.sharding import PartitionSpec as P

epsilon = 1e-05


def normalize(values, channel_dim):
    values = values.astype(jnp.float32)
    centred = values - jnp.mean(values, axis=channel_dim, keepdims=True)
    spread = jnp.mean(centred * centred, axis=channel_dim, keepdims=True)
    return centred * lax.rsqrt(spread + epsilon)


def gather_kernel(n_row, n_col, count, *refs):
    blocks, outs = refs[:count], refs[count : 2 * count]
    own_sem, send_sems, far_sems, recv_sems = refs[2 * count :]
    span = n_row // n_col
    row = lax.axis_index("row")
    col = lax.axis_index("col")
    band = row // span
    place = lax.rem(row, span)
    parity = lax.rem(place, 2)
    base = band * span
    twin_place = place + 1 - 2 * parity
    is_source = band == col
    half = span // 2

    def other_band(k):
        return lax.rem(band + k, n_col) * span + place

    def peer_place(k):
        return lax.rem(place + 2 * k, span)

    barrier = pltpu.get_barrier_semaphore()
    for k in range(1, n_col):
        pl.semaphore_signal(barrier, inc=1, device_id={"row": other_band(k)})
    pl.semaphore_signal(barrier, inc=1, device_id={"row": base + twin_place})
    for k in range(1, half):
        pl.semaphore_signal(barrier, inc=1, device_id={"row": base + peer_place(k)})
    pl.semaphore_wait(barrier, n_col - 1 + half)

    def push(n, source, slot, sem, target):
        return pltpu.make_async_remote_copy(
            src_ref=source,
            dst_ref=outs[n].at[slot],
            send_sem=sem,
            recv_sem=recv_sems.at[n, slot],
            device_id={"row": target},
        )

    def far(n, k):
        return push(n, blocks[n], place, far_sems.at[n, k - 1], other_band(k))

    def own_copy(n):
        return pltpu.make_async_copy(blocks[n], outs[n].at[place], own_sem.at[n])

    def arrival(n, slot):
        return push(n, outs[n].at[place], slot, own_sem.at[n], base + twin_place)

    @pl.when(is_source)
    def _():
        for n in range(count):
            for k in range(1, n_col):
                far(n, k).start()
            own_copy(n).start()
        for n in range(count):
            own_copy(n).wait()

    sent = []
    for n in range(count):

        @pl.when(jnp.logical_not(is_source))
        def _():
            arrival(n, place).wait_recv()

        mine = outs[n].at[place]
        near = [
            push(n, mine, place, send_sems.at[n, k - 1], base + peer_place(k))
            for k in range(1, half)
        ]
        near.append(push(n, mine, place, send_sems.at[n, half - 1], base + twin_place))
        for copy in near:
            copy.start()
        sent += near
    for n in range(count):
        for k in range(1, half):
            came = lax.rem(place - 2 * k + span, span)
            arrival(n, came).wait_recv()
            onward = push(
                n, outs[n].at[came], came, send_sems.at[n, half - 1 + k], base + twin_place
            )
            onward.start()
            sent.append(onward)
    for n in range(count):
        for k in range(half):
            arrival(n, lax.rem(twin_place + 2 * k, span)).wait_recv()
    for copy in sent:
        copy.wait_send()

    @pl.when(is_source)
    def _():
        for n in range(count):
            for k in range(1, n_col):
                far(n, k).wait_send()


def gather_blocks(*blocks):
    n_row = lax.axis_size("row")
    n_col = lax.axis_size("col")
    span = n_row // n_col
    count = len(blocks)
    return pl.pallas_call(
        functools.partial(gather_kernel, n_row, n_col, count),
        out_shape=tuple(
            jax.ShapeDtypeStruct((span,) + block.shape, block.dtype) for block in blocks
        ),
        in_specs=[pl.BlockSpec(memory_space=pltpu.VMEM)] * count,
        out_specs=tuple(pl.BlockSpec(memory_space=pltpu.VMEM) for _ in blocks),
        scratch_shapes=[
            pltpu.SemaphoreType.DMA((count,)),
            pltpu.SemaphoreType.DMA((count, span)),
            pltpu.SemaphoreType.DMA((count, max(n_col - 1, 1))),
            pltpu.SemaphoreType.DMA((count, span)),
        ],
        compiler_params=pltpu.CompilerParams(collective_id=0, has_side_effects=True),
        name="gather_blocks",
    )(*blocks)


def sum_columns(values, wire_dtype):
    n_col = lax.axis_size("col")
    total = values
    sent = values.astype(wire_dtype)
    for shift in range(1, n_col):
        pairs = [(k, (k + shift) % n_col) for k in range(n_col)]
        total = total + lax.ppermute(sent, "col", pairs).astype(jnp.float32)
    return total


def product_kernel(n_row, n_col, tok_row, tok_col, received_ref, out_ref, left_ref, right_ref):
    for r in range(n_row):
        for u in range(n_col):
            rows = slice(r * tok_row, (r + 1) * tok_row)
            lanes = slice(u * tok_col, (u + 1) * tok_col)
            left_ref[rows, lanes] = received_ref[r * n_col + u, 0, 0]
            right_ref[rows, lanes] = received_ref[r * n_col + u, 1, 0]
    result = lax.dot_general(
        left_ref[...], right_ref[...], (((1,), (1,)), ((), ())), preferred_element_type=jnp.float32
    ).astype(jnp.bfloat16)
    for r in range(n_row):
        for u in range(n_col):
            rows = slice(r * tok_row, (r + 1) * tok_row)
            lanes = slice(u * tok_col, (u + 1) * tok_col)
            out_ref[r * n_col + u, 0] = result[rows, lanes]


def triangle_product(received, n_row, n_col):
    devices, _, items, tok_row, tok_col = received.shape
    length = n_row * tok_row
    return pl.pallas_call(
        functools.partial(product_kernel, n_row, n_col, tok_row, tok_col),
        grid=(items,),
        out_shape=jax.ShapeDtypeStruct((devices, items, tok_row, tok_col), jnp.bfloat16),
        in_specs=[
            pl.BlockSpec((devices, 2, 1, tok_row, tok_col), lambda c: (0, 0, c, 0, 0))
        ],
        out_specs=pl.BlockSpec((devices, 1, tok_row, tok_col), lambda c: (0, c, 0, 0)),
        scratch_shapes=[
            pltpu.VMEM((length, length), jnp.bfloat16),
            pltpu.VMEM((length, length), jnp.bfloat16),
        ],
        name="triangle_product",
    )(received)


def prep_kernel(
    index_ref, pool_ref, proj_ref, align_ref, norm_ref, flat_ref, row_ref, column_ref, held_ref
):
    tok_row, align_width, stored = pool_ref.shape
    samples = align_ref.shape[1]
    outer_width = proj_ref.shape[1] // 2
    half = outer_width // 2
    slots = lax.broadcasted_iota(jnp.int32, (stored, samples), 0)
    picks = (slots == index_ref[...]).astype(jnp.float32).T.astype(jnp.bfloat16)
    lanes = lax.broadcasted_iota(jnp.int32, (half, 2 * samples), 1)
    row_weight = proj_ref[:, :outer_width]
    column_weight = proj_ref[...].astype(jnp.float32).T[outer_width:].astype(jnp.bfloat16)
    for t in range(tok_row):
        chosen = lax.dot_general(
            picks, pool_ref[t], (((1,), (1,)), ((), ())), preferred_element_type=jnp.float32
        )
        normed = normalize(chosen, 1).astype(jnp.bfloat16)
        align_ref[t] = chosen.astype(jnp.bfloat16)
        norm_ref[t] = normed
        flat_ref[:, t * align_width : (t + 1) * align_width] = normed
        row_ref[t * samples : (t + 1) * samples, :] = jnp.dot(
            normed, row_weight, preferred_element_type=jnp.float32
        ).astype(jnp.bfloat16)
        factor = lax.dot_general(
            column_weight,
            jnp.concatenate([normed, normed], axis=0),
            (((1,), (1,)), ((), ())),
            preferred_element_type=jnp.float32,
        )
        held_ref[t * half : (t + 1) * half, :] = jnp.where(
            lanes < samples, factor[:half], factor[half:]
        )
    for d in range(half):
        column_ref[:, d * 2 * samples : (d + 1) * 2 * samples] = held_ref[
            pl.ds(d, tok_row, stride=half), :
        ].astype(jnp.bfloat16)


def prepare(alignment_pool, sample_index, outer_proj):
    stored, tok_row, align_width = alignment_pool.shape
    samples = sample_index.shape[0]
    outer_width = outer_proj.shape[1] // 2
    half = outer_width // 2
    return pl.pallas_call(
        prep_kernel,
        out_shape=(
            jax.ShapeDtypeStruct((tok_row, samples, align_width), jnp.bfloat16),
            jax.ShapeDtypeStruct((tok_row, samples, align_width), jnp.bfloat16),
            jax.ShapeDtypeStruct((samples, tok_row * align_width), jnp.bfloat16),
            jax.ShapeDtypeStruct((tok_row * samples, outer_width), jnp.bfloat16),
            jax.ShapeDtypeStruct((tok_row, outer_width * samples), jnp.bfloat16),
        ),
        scratch_shapes=[pltpu.VMEM((tok_row * half, 2 * samples), jnp.float32)],
        name="prepare",
    )(sample_index[None, :], alignment_pool.transpose(1, 2, 0), outer_proj)


def pair_kernel(
    steps,
    step_rows,
    samples,
    head_count,
    column_ref,
    row_ref,
    mix_ref,
    grid_ref,
    proj_ref,
    logit_ref,
    mark_ref,
    mask_ref,
    one_ref,
    norm_ref,
    score_ref,
    factor_ref,
    held_ref,
    wide_ref,
    mixed_ref,
    weight_ref,
):
    step = pl.program_id(0)
    pair_width = grid_ref.shape[2]
    outer_width = row_ref.shape[1]
    half = outer_width // 2
    tok_row = steps * step_rows
    order = [side * half + d for d in range(half) for side in range(2)]

    @pl.when(step == 0)
    def _():
        wide_ref[...] = mix_ref[...].astype(jnp.float32)
        for d in range(outer_width):
            mixed_ref[:, d * pair_width : (d + 1) * pair_width] = wide_ref[
                pl.ds(d, outer_width, stride=outer_width), :
            ].astype(jnp.bfloat16)
        for n in range(4):
            part = proj_ref[:, n * pair_width : (n + 1) * pair_width].astype(jnp.float32)
            weight_ref[n * pair_width : (n + 1) * pair_width, :] = part.T.astype(jnp.bfloat16)
        weight_ref[4 * pair_width :, :] = logit_ref[...]

    tok_col = grid_ref.shape[1]
    row_start = lax.axis_index("row") * tok_row
    column_start = pl.multiple_of(lax.axis_index("col") * tok_col, tok_col)
    column_mask = mask_ref[:, pl.ds(column_start, tok_col)].astype(jnp.float32)
    spread = jnp.dot(row_ref[...], mixed_ref[...], preferred_element_type=jnp.float32).astype(
        jnp.bfloat16
    )
    updates = []
    for first in range(0, step_rows, 2):
        both = []
        for k in range(first, min(first + 2, step_rows)):
            piece = spread[k * samples : (k + 1) * samples]
            both.append(
                jnp.concatenate(
                    [piece[:, d * pair_width : (d + 1) * pair_width] for d in order], axis=0
                )
            )
        update = jnp.dot(
            column_ref[...], jnp.concatenate(both, axis=1), preferred_element_type=jnp.float32
        )
        for k in range(len(both)):
            updates.append(update[:, k * pair_width : (k + 1) * pair_width])
    for k in range(step_rows):
        update = updates[k]
        pair_one = (grid_ref[k].astype(jnp.float32) + update * (1.0 / samples)).astype(jnp.bfloat16)
        one_ref[k] = pair_one
        pair_norm = normalize(pair_one, 1).astype(jnp.bfloat16)
        norm_ref[k] = pair_norm
        projected = lax.dot_general(
            weight_ref[...],
            pair_norm,
            (((1,), (1,)), ((), ())),
            preferred_element_type=jnp.float32,
        )
        row = step * step_rows + k
        mask = column_mask * mark_ref[row_start + row].astype(jnp.float32)
        for side in range(2):
            base = 2 * side * pair_width
            gate = projected[base : base + pair_width]
            value = projected[base + pair_width : base + 2 * pair_width]
            held_ref[side, pl.ds(row, pair_width, stride=tok_row), :] = (
                jax.nn.sigmoid(gate) * value * mask
            )
        score_ref[k] = jnp.exp(projected[4 * pair_width : 4 * pair_width + head_count])

    @pl.when(step == steps - 1)
    def _():
        devices, _, group, _, tok_col = factor_ref.shape
        for side in range(2):
            factor_ref[:, side] = (
                held_ref[side].astype(jnp.bfloat16).reshape(devices, group, tok_row, tok_col)
            )


def pair_stage(columns, rows, outer_mix, pair_grid, triangle_proj, pair_logit, token_mask, devices):
    tok_row, tok_col, pair_width = pair_grid.shape
    outer_width = rows.shape[1]
    samples = rows.shape[0] // tok_row
    head_count = pair_logit.shape[1]
    step_rows = 4 if tok_row % 4 == 0 else 1
    steps = tok_row // step_rows
    group = pair_width // devices
    whole = lambda *shape: pl.BlockSpec(shape, lambda r: (0,) * len(shape))
    part = lambda *shape: pl.BlockSpec(shape, lambda r: (r,) + (0,) * (len(shape) - 1))
    return pl.pallas_call(
        functools.partial(pair_kernel, steps, step_rows, samples, head_count),
        grid=(steps,),
        out_shape=(
            jax.ShapeDtypeStruct(pair_grid.shape, jnp.bfloat16),
            jax.ShapeDtypeStruct(pair_grid.shape, jnp.bfloat16),
            jax.ShapeDtypeStruct((tok_row, head_count, tok_col), jnp.float32),
            jax.ShapeDtypeStruct((devices, 2, group, tok_row, tok_col), jnp.bfloat16),
        ),
        in_specs=[
            whole(*columns.shape),
            part(step_rows * samples, outer_width),
            whole(*outer_mix.shape),
            part(step_rows, tok_col, pair_width),
            whole(*triangle_proj.shape),
            whole(*pair_logit.shape[::-1]),
            pl.BlockSpec(memory_space=pltpu.SMEM),
            whole(1, token_mask.shape[0]),
        ],
        out_specs=(
            part(step_rows, tok_col, pair_width),
            part(step_rows, tok_col, pair_width),
            part(step_rows, head_count, tok_col),
            whole(devices, 2, group, tok_row, tok_col),
        ),
        scratch_shapes=[
            pltpu.VMEM((2, pair_width * tok_row, tok_col), jnp.float32),
            pltpu.VMEM(outer_mix.shape, jnp.float32),
            pltpu.VMEM((outer_width, outer_width * pair_width), jnp.bfloat16),
            pltpu.VMEM((4 * pair_width + head_count, pair_width), jnp.bfloat16),
        ],
        name="pair_stage",
    )(columns, rows, outer_mix, pair_grid, triangle_proj, pair_logit.T, token_mask, token_mask[None, :])


def tail_kernel(
    step_rows, product_ref, one_ref, gate_ref, mix_ref, up_ref, down_ref, out_ref, held_ref
):
    step = pl.program_id(0)
    devices, group, tok_row, tok_col = product_ref.shape
    pair_width = devices * group
    inner_width = down_ref.shape[0]

    @pl.when(step == 0)
    def _():
        held_ref[...] = (
            product_ref[...].astype(jnp.float32).reshape(pair_width * tok_row, tok_col)
        )

    rows = []
    for k in range(step_rows):
        product = held_ref[pl.ds(step * step_rows + k, pair_width, stride=tok_row), :]
        normed = normalize(product, 0).astype(jnp.bfloat16)
        mixed = lax.dot_general(
            normed, mix_ref[...], (((0,), (0,)), ((), ())), preferred_element_type=jnp.float32
        )
        rows.append((one_ref[k].astype(jnp.float32) + gate_ref[k] * mixed).astype(jnp.bfloat16))
    pair_two = jnp.concatenate(rows, axis=0)
    normed = normalize(pair_two, 1).astype(jnp.bfloat16)
    expanded = jnp.dot(normed, up_ref[...], preferred_element_type=jnp.float32)
    hidden = (jax.nn.silu(expanded[:, :inner_width]) * expanded[:, inner_width:]).astype(
        jnp.bfloat16
    )
    result = (
        pair_two.astype(jnp.float32)
        + jnp.dot(hidden, down_ref[...], preferred_element_type=jnp.float32)
    ).astype(jnp.bfloat16)
    for k in range(step_rows):
        out_ref[k] = result[k * tok_col : (k + 1) * tok_col]


def tail_stage(product, pair_one, gate_out, triangle_mix, transition_up, transition_down):
    tok_row, tok_col, pair_width = pair_one.shape
    step_rows = 4 if tok_row % 4 == 0 else 1
    whole = lambda *shape: pl.BlockSpec(shape, lambda r: (0,) * len(shape))
    part = lambda *shape: pl.BlockSpec(shape, lambda r: (r,) + (0,) * (len(shape) - 1))
    block = part(step_rows, tok_col, pair_width)
    return pl.pallas_call(
        functools.partial(tail_kernel, step_rows),
        grid=(tok_row // step_rows,),
        out_shape=jax.ShapeDtypeStruct(pair_one.shape, jnp.bfloat16),
        in_specs=[
            whole(*product.shape),
            block,
            block,
            whole(*triangle_mix.shape),
            whole(*transition_up.shape),
            whole(*transition_down.shape),
        ],
        out_specs=block,
        scratch_shapes=[pltpu.VMEM((pair_width * tok_row, tok_col), jnp.float32)],
        name="tail_stage",
    )(product, pair_one, gate_out, triangle_mix, transition_up, transition_down)


def on_device(
    pair_grid,
    alignment_pool,
    sample_index,
    token_mask,
    outer_proj,
    outer_mix,
    pair_logit,
    average_proj,
    average_mix,
    triangle_proj,
    triangle_mix,
    transition_up,
    transition_down,
):
    n_row = lax.axis_size("row")
    n_col = lax.axis_size("col")
    tok_row = pair_grid.shape[0]
    tok_col = pair_grid.shape[1]
    pair_width = pair_grid.shape[2]
    samples = sample_index.shape[0]
    align_width = alignment_pool.shape[2]
    head_count = pair_logit.shape[1]
    head_total = average_proj.shape[1] // 2
    head_dim = head_total // head_count
    alignments, align_norm, align_rows, rows, column_block = prepare(
        alignment_pool, sample_index, outer_proj
    )
    columns, gathered = gather_blocks(column_block, align_rows)
    columns = columns.reshape(tok_col, column_block.shape[1])
    pair_one, pair_norm, weights, factors = pair_stage(
        columns,
        rows,
        outer_mix,
        pair_grid,
        triangle_proj,
        pair_logit,
        token_mask,
        n_row * n_col,
    )
    received = lax.all_to_all(factors, ("row", "col"), split_axis=0, concat_axis=0, tiled=True)
    column_norm = (
        gathered.reshape(n_row // n_col, samples, tok_row, align_width)
        .transpose(1, 0, 2, 3)
        .reshape(samples, tok_col, align_width)
    )
    value_weight = average_proj[:, :head_total].reshape(align_width, head_count, head_dim)
    gate_weight = average_proj[:, head_total:].reshape(align_width, head_count, head_dim)
    mix_weight = average_mix.reshape(head_count, head_dim, align_width)
    weights = weights.transpose(1, 0, 2)
    partial_total = jnp.sum(weights, axis=2)
    weights_low = weights.astype(jnp.bfloat16)
    column_values = jnp.einsum(
        "sjm,mhc->hjsc", column_norm, value_weight, preferred_element_type=jnp.float32
    )
    column_values = column_values.astype(jnp.bfloat16).reshape(
        head_count, tok_col, samples * head_dim
    )
    partial_sum = jnp.einsum(
        "hij,hjk->hik", weights_low, column_values, preferred_element_type=jnp.float32
    )
    partial_sum = partial_sum.astype(jnp.bfloat16)
    received, partial_sum, partial_total = lax.optimization_barrier(
        (received, partial_sum, partial_total)
    )
    weighted = sum_columns(partial_sum, jnp.bfloat16)
    totals = sum_columns(partial_total, jnp.float32)
    gate_values = jax.nn.sigmoid(
        jnp.einsum("ism,mhc->hisc", align_norm, gate_weight, preferred_element_type=jnp.float32)
    )
    weighted = weighted.reshape(head_count, tok_row, samples, head_dim)
    averaged = (gate_values * weighted / totals[:, :, None, None]).astype(jnp.bfloat16)
    align_update = jnp.einsum(
        "hisc,hcm->sim", averaged, mix_weight, preferred_element_type=jnp.float32
    )
    alignment_next = (
        alignments.transpose(1, 0, 2).astype(jnp.float32) + align_update
    ).astype(jnp.bfloat16)
    flat_result = triangle_product(received, n_row, n_col)
    flat_result, late_norm = lax.optimization_barrier((flat_result, pair_norm))
    product = lax.all_to_all(flat_result, ("row", "col"), split_axis=0, concat_axis=0, tiled=True)
    gate_out = jax.nn.sigmoid(
        jnp.dot(late_norm, triangle_proj[:, 4 * pair_width :], preferred_element_type=jnp.float32)
    )
    pair_next = tail_stage(
        product, pair_one, gate_out, triangle_mix, transition_up, transition_down
    )
    return (pair_next, alignment_next)


def solution(mesh):
    in_specs = (
        P(("groups", "row"), "col", None),
        P("groups", "row", None),
        P("groups"),
        P("groups"),
        P(),
        P(),
        P(),
        P(),
        P(),
        P(),
        P(),
        P(),
        P(),
    )
    out_specs = (P(("groups", "row"), "col", None), P("groups", "row", None))
    return jax.shard_map(
        on_device, mesh=mesh, in_specs=in_specs, out_specs=out_specs, check_vma=False
    )
```
